256 devices in a mesh: tile: 8 (over y, core), freq: 32 (over x, z).
Axes of the slice: x: 4, y: 4, z: 8, core: 2. Of those that a mesh axis runs over, the one named last changes fastest.
Arguments:
- sensitivity: float32 [8, 32, 2, 1024, 512], P('tile', 'freq'), may hold values from -0.25 to 0.25
- models: float32 [2048, 256], P(('tile', 'freq')), may hold values from -6 to 6
- observed: float32 [8, 40, 1024], P('tile', None, 'freq'), may hold values from -6 to 6
- waveform: float32 [128], replicated, may hold values from -0.5 to 0.5
- cell_index: int32 [8, 512], P('tile'), may hold values from 0 to 2047, as said below
- gate_index: int32 [40], replicated, may hold values from 10 to 127, as said below
Outputs:
- updated: float32 [2048, 256], P(('tile', 'freq'))
- misfit: float32 [256], replicated
The draws below stay inside these ranges and needn't reach their ends.
Inputs may be any that keep to these rules, and one draw needn't show every extreme that they name: `cell_index`: each tile's indices are distinct. Tile t holds, in some order, the 256 global cells from t * 256 on and the 256 cells of one other tile's block (from u * 256 on, u != t). Every global cell belongs to one or more tiles. `gate_index`: strictly increasing; the last gate is sample 128 - 1.
All inputs are finite; a program needn't handle non-finite values.
Results may differ from the reference program's by a relative error of at most 0.00017.
Values sent between devices are 32-bit elements; how exact they have to be, the bound alone decides.
A program may use at most 64 MiB of HBM per device.

```python
import math
import jax
import jax.numpy as jnp
from jax import lax

FREQS = 32
GATES = 40
SAMPLES = 128
SOUND = 1024
CELLS = 512
MEMBERS = 256
TILES = 8
NCELL = 2048


def draw_cell_index(key, part):
    half = CELLS // 2
    first_key = jax.random.fold_in(key, 11)
    second_key = jax.random.fold_in(key, 23)
    shifts = jax.random.randint(first_key, (TILES,), 0, TILES - 1)
    others = (jnp.arange(TILES) + 1 + shifts) % TILES
    within = jnp.arange(half)[None, :]
    owned = jnp.arange(TILES)[:, None] * half + within
    borrowed = others[:, None] * half + within
    joined = jnp.concatenate([owned, borrowed], axis=1)
    orders = jax.vmap(lambda k: jax.random.permutation(k, CELLS))(jax.random.split(second_key, TILES))
    return jnp.take_along_axis(joined, orders, axis=1).astype(jnp.int32)


def draw_gate_index(key, part):
    spacing = jax.random.randint(jax.random.fold_in(key, 5), (GATES,), 1, 4)
    after = jnp.cumsum(spacing[::-1])[::-1] - spacing
    return (SAMPLES - 1 - after).astype(jnp.int32)


def levels(key, dims, cuts, low, largest):
    def one(dim, shards_of):
        draws = jax.random.uniform(jax.random.fold_in(jax.random.fold_in(key, 6), dim), (shards_of,), jnp.float32, low / len(cuts), largest / len(cuts))
        return jnp.repeat(jnp.exp(draws), dims[dim] // shards_of).reshape((-1,) + (1,) * (len(dims) - dim - 1))

    gain = one(*cuts[0])
    for cut in cuts[1:]:
        gain = gain * one(*cut)
    return gain


def scatter_about(stream_key, extent, deviation, bound, shards=(), kind=jnp.bfloat16):
    loudness = levels(stream_key, extent, shards, -0.22, 0.18) if shards else 1.0
    values = jax.random.normal(stream_key, extent, jnp.float32) * deviation * loudness
    return jnp.minimum(jnp.maximum(values, -bound), bound).astype(kind)


def setup_inputs(seed: int = 0) -> dict:
    seeds = jax.random.split(jax.random.key(seed), 7)
    return {
        "sensitivity": scatter_about(seeds[0], (TILES, FREQS, 2, SOUND, CELLS), CELLS ** -0.5, 0.25, ((0, 8), (1, 32)), jnp.float32),
        "models": scatter_about(seeds[1], (NCELL, MEMBERS), 1.0, 6.0, ((0, 256),), jnp.float32),
        "observed": scatter_about(seeds[2], (TILES, GATES, SOUND), 1.0, 6.0, ((0, 8), (2, 32)), jnp.float32),
        "waveform": scatter_about(seeds[3], (SAMPLES,), SAMPLES ** -0.5, 0.5, (), jnp.float32),
        "cell_index": draw_cell_index(jax.random.fold_in(seeds[6], 71), 0),
        "gate_index": draw_gate_index(jax.random.fold_in(seeds[6], 71), 0),
    }


HIGH = lax.Precision.HIGHEST
PHASE_RATE = 0.37
STEP_LENGTH = 0.5
EPSILON = 1e-06

def gate_tables(freqs, waveform, gate_index):
    samples = waveform.shape[0]
    freq_col = jnp.arange(freqs, dtype=jnp.float32)[:, None] + 0.5
    time_row = jnp.arange(samples, dtype=jnp.float32)[None, :] + 0.5
    phases = PHASE_RATE * freq_col * time_row
    kernel = jnp.stack([jnp.cos(phases), jnp.sin(phases)], axis=1) / math.sqrt(freqs)
    time_lag = jnp.arange(samples)[:, None] - jnp.arange(samples)[None, :]
    toeplitz = jnp.where(time_lag >= 0, jnp.take(waveform, jnp.clip(time_lag, 0, samples - 1)), 0.0)
    picker = (gate_index[:, None] == jnp.arange(samples)[None, :]).astype(jnp.float32)
    return (kernel, toeplitz, picker)

def reference(sensitivity, models, observed, waveform, cell_index, gate_index):
    freqs = sensitivity.shape[1]
    members = models.shape[1]
    total = sensitivity.shape[0] * sensitivity.shape[3] * gate_index.shape[0]
    kernel, toeplitz, picker = gate_tables(freqs, waveform, gate_index)

    def per_tile(pieces):
        block, cells, seen = pieces
        tile_models = jnp.take(models, cells, axis=0)
        predicted = jnp.einsum('fpsc,cm->fpsm', block, tile_models, precision=HIGH)
        series = jnp.einsum('fpk,fpsm->ksm', kernel, predicted, precision=HIGH)
        series = jnp.einsum('kj,jsm->ksm', toeplitz, series, precision=HIGH)
        response = jnp.einsum('gk,ksm->gsm', picker, series, precision=HIGH)
        misfit_rows = response - seen[:, :, None]
        upward = jnp.einsum('gk,gsm->ksm', picker, misfit_rows, precision=HIGH)
        upward = jnp.einsum('kj,ksm->jsm', toeplitz, upward, precision=HIGH)
        back = jnp.einsum('fpk,ksm->fpsm', kernel, upward, precision=HIGH)
        cell_terms = jnp.einsum('fpsc,fpsm->cm', block, back, precision=HIGH)
        return (cell_terms, lax.optimization_barrier(jnp.sum(misfit_rows * misfit_rows, axis=(0, 1))))
    cell_terms, squares = lax.map(per_tile, (sensitivity, cell_index, observed))
    gradient = jnp.zeros_like(models).at[cell_index.reshape(-1)].add(cell_terms.reshape(-1, members))
    misfit = lax.optimization_barrier(jnp.sum(squares, axis=0)) / (2.0 * total)
    scale = jnp.sqrt(lax.optimization_barrier(jnp.mean(gradient * gradient, axis=0)) + EPSILON)
    updated = models - STEP_LENGTH * (misfit / scale)[None, :] * gradient
    return (updated, misfit)
```

```python
import functools
import math

import jax
import jax.numpy as jnp
import numpy as np
from jax import lax
from jax.experimental import pallas as pl
from jax.experimental.pallas import tpu as pltpu
from jax.sharding import PartitionSpec as P

HIGH = lax.Precision.HIGHEST
PHASE_RATE = 0.37
STEP_LENGTH = 0.5
EPSILON = 1e-06
MESH = pl.DeviceIdType.MESH
NX, NZ, NT = 4, 8, 8
NF = NX * NZ
ROWS = 8
F32, BF16 = jnp.float32, jnp.bfloat16


def kernel_table(freqs, samples):
    freq_col = np.arange(freqs, dtype=np.float32)[:, None] + np.float32(0.5)
    time_row = np.arange(samples, dtype=np.float32)[None, :] + np.float32(0.5)
    phases = ((np.float32(PHASE_RATE) * freq_col) * time_row).astype(np.float64)
    table = np.stack([np.cos(phases), np.sin(phases)], axis=1) / math.sqrt(freqs)
    return table.reshape(2 * freqs, samples).astype(np.float32)


def nn(a, b, precision=None):
    return lax.dot_general(a, b, (((1,), (0,)), ((), ())), precision=precision, preferred_element_type=F32)


def nt(a, b, precision=None):
    return lax.dot_general(a, b, (((1,), (1,)), ((), ())), precision=precision, preferred_element_type=F32)


def split(a):
    high = a.astype(BF16)
    return high, (a - high.astype(F32)).astype(BF16)


def three(dot, a, b):
    return dot(a[0], b[0]) + dot(a[0], b[1]) + dot(a[1], b[0])


def iota(shape, dim):
    return lax.broadcasted_iota(jnp.int32, shape, dim)


def await_bytes(ref, sem):
    pltpu.make_async_copy(ref, ref, sem).wait()


def kernel(
    wave_ref, gate_ref, sens_ref, models_ref, obs_ref, cell_ref, table_ref,
    out_ref, misfit_ref,
    buf, tiles, gathered, wide, expanded, onehot, model_t, cells_t, grads, xrecv, zsend, zrecv, tsend, trecv,
    square_row, square_rows, misfit_row, misfit_rows, final_row, final_rows,
    bulk_send, bulk_recv, send, recv, pair_send, pair_recv,
):
    tile = lax.axis_index("tile")
    f = lax.axis_index("freq")
    x, z = f // NZ, lax.rem(f, NZ)
    chunks = buf.shape[0]
    soundings = chunks * ROWS
    gates = obs_ref.shape[1]
    total = NT * NF * soundings * gates
    ncells = NT * NF * ROWS

    def plane(i):
        return {"freq": lax.rem(x + i // NZ, NX) * NZ + lax.rem(z + i % NZ, NZ)}

    def other_tile(i):
        return {"tile": lax.rem(tile + i, NT)}

    def put(src, dst, send_sem, recv_sem, device):
        pltpu.make_async_remote_copy(
            src_ref=src, dst_ref=dst, send_sem=send_sem, recv_sem=recv_sem, device_id=device, device_id_type=MESH
        ).start()

    barrier = pltpu.get_barrier_semaphore()
    for i in range(1, NF):
        pl.semaphore_signal(barrier, inc=1, device_id=plane(i), device_id_type=MESH)
    for i in range(1, NT):
        pl.semaphore_signal(barrier, inc=1, device_id=other_tile(i), device_id_type=MESH)
    pl.semaphore_wait(barrier, NF + NT - 2)

    for i in range(1, NT):
        put(models_ref, tiles.at[tile], send.at[0], recv.at[0], other_tile(i))

    def send_chunk(c):
        for i in range(1, NF):
            p = plane(i)
            start = pl.multiple_of(p["freq"] * soundings + c * ROWS, ROWS)
            put(sens_ref.at[0, 0, :, pl.ds(start, ROWS), :], buf.at[c, f], bulk_send.at[c], bulk_recv.at[c], p)
        start = pl.multiple_of(f * soundings + c * ROWS, ROWS)
        pltpu.make_async_copy(sens_ref.at[0, 0, :, pl.ds(start, ROWS), :], buf.at[c, f], bulk_recv.at[c]).start()

    send_chunk(0)

    cells = cell_ref[...]
    block = lax.shift_right_logical(cells, 8)
    partner = jnp.max(jnp.where(block != tile, block, -1), axis=1, keepdims=True)
    local = jnp.where(block == tile, cells & 255, 256 + (cells & 255))
    ncell = cells.shape[1]
    onehot[...] = jnp.where(iota((ncell, ncell), 0) == local, 1.0, 0.0).astype(BF16)

    tiles[tile] = models_ref[...]
    await_bytes(tiles.at[pl.ds(0, NT - 1)], recv.at[0])
    borrowed = jnp.zeros_like(models_ref)
    for t in range(NT):
        borrowed = jnp.where(partner == t, tiles[t], borrowed)
    gathered[x, z, 0] = models_ref[...]
    gathered[x, z, 1] = borrowed
    for i in range(1, NZ):
        put(gathered.at[x, z], gathered.at[x, z], send.at[1], recv.at[1], plane(i))
    send_chunk(1)

    samples = table_ref.shape[1]
    rows = iota((gates, samples), 0)
    lag = lax.fori_loop(0, gates, lambda g, a: jnp.where(rows == g, gate_ref[g], a), jnp.zeros((gates, samples), jnp.int32))
    lag = lag - iota((gates, samples), 1)
    toeplitz = lax.fori_loop(
        0, samples, lambda k, a: jnp.where(lag == k, wave_ref[k], a), jnp.zeros((gates, samples), F32)
    )
    narrow = nt(toeplitz, table_ref[...], HIGH)
    spread = jnp.where(lax.shift_right_logical(iota((gates * ROWS, gates), 0), 3) == iota((gates * ROWS, gates), 1), 1.0, 0.0)
    fps = narrow.shape[1]
    pick = jnp.where(iota((fps, fps * ROWS), 0) == lax.shift_right_logical(iota((fps, fps * ROWS), 1), 3), 1.0, 0.0)
    big = nn(nn(spread, narrow, HIGH), pick, HIGH)
    same = (iota(big.shape, 0) & 7) == (iota(big.shape, 1) & 7)
    big_high, big_low = split(jnp.where(same, big, 0.0))
    wide[0] = big_high
    wide[1] = big_low
    expanded[...] = nn(spread, obs_ref[0], HIGH)

    await_bytes(gathered.at[0, pl.ds(0, NZ - 1)], recv.at[1])
    for i in range(1, NX):
        put(gathered.at[x], gathered.at[x], send.at[2], recv.at[2], plane(i * NZ))
    send_chunk(2)
    send_chunk(3)

    await_bytes(gathered.at[pl.ds(0, NX - 1)], recv.at[2])
    for b in range(2):
        part = gathered[:, :, b].reshape(NF * ROWS, -1)
        part_high, part_low = split(part.T)
        hot = onehot[pl.ds(b * NF * ROWS, NF * ROWS), :]
        if b == 0:
            model_high, model_low = nn(part_high, hot), nn(part_low, hot)
        else:
            model_high, model_low = model_high + nn(part_high, hot), model_low + nn(part_low, hot)
    model_t[0] = model_high.astype(BF16)
    model_t[1] = model_low.astype(BF16)

    cells_t[...] = jnp.zeros_like(cells_t)
    misfit_row[...] = jnp.zeros_like(misfit_row)

    def chunk(c, carry):
        await_bytes(buf.at[c], bulk_recv.at[c])
        block_s = split(buf[c].reshape(fps * ROWS, ncell))
        operator = split(three(nn, (wide[0], wide[1]), block_s))
        seen = expanded[...]
        seen = jnp.where(iota(seen.shape, 1) == c * ROWS + (iota(seen.shape, 0) & 7), seen, 0.0)
        seen_row = nt(jnp.ones((8, seen.shape[1]), F32), seen, HIGH)[0:1]
        rows_t = three(nt, (model_t[0], model_t[1]), operator) - seen_row
        misfit_row[...] += nt(jnp.ones((8, rows_t.shape[1]), F32), rows_t * rows_t, HIGH)[0:1]
        cells_t[...] += three(nn, split(rows_t), operator)
        return carry

    lax.fori_loop(0, chunks, chunk, 0)

    grad_high, grad_low = split(cells_t[...])
    half = NF * ROWS
    for b in (1, 0):
        hot = onehot[pl.ds(b * half, half), :]
        part = nt(hot, grad_high) + nt(hot, grad_low)
        grads[b] = part.reshape(NX, NZ, ROWS, -1)
        for i in range(1, NX):
            p = lax.rem(x + i, NX)
            put(grads.at[b, p], xrecv.at[b, x], pair_send.at[0, b], pair_recv.at[0, b], plane(i * NZ))
    for i in range(1, NF):
        put(misfit_row, misfit_rows.at[f], send.at[3], recv.at[3], plane(i))
    for b in (1, 0):
        xrecv[b, x] = grads[b, x]
        await_bytes(xrecv.at[b, pl.ds(0, NX - 1)], pair_recv.at[0, b])
        zsend[b] = (xrecv[b, 0] + xrecv[b, 1]) + (xrecv[b, 2] + xrecv[b, 3])
        for i in range(1, NZ):
            p = lax.rem(z + i, NZ)
            put(zsend.at[b, p], zrecv.at[b, z], pair_send.at[1, b], pair_recv.at[1, b], plane(i))
    sums = []
    for b in (1, 0):
        zrecv[b, z] = zsend[b, z]
        await_bytes(zrecv.at[b, pl.ds(0, NZ - 1)], pair_recv.at[1, b])
        sums.append(jnp.sum(zrecv[b], axis=0))
        if b == 1:
            for t in range(NT):
                tsend[t] = jnp.where(partner == t, sums[0], 0.0)
            for i in range(1, NT):
                put(tsend.at[lax.rem(tile + i, NT)], trecv.at[tile], send.at[4], recv.at[4], other_tile(i))
    trecv[tile] = jnp.zeros_like(sums[0])
    await_bytes(trecv.at[pl.ds(0, NT - 1)], recv.at[4])
    gradient = sums[1] + jnp.sum(trecv[...], axis=0)

    square_row[...] = jnp.sum(gradient * gradient, axis=0, keepdims=True)
    for i in range(1, NF):
        put(square_row, square_rows.at[f], send.at[5], recv.at[5], plane(i))
    square_rows[f] = square_row[...]
    misfit_rows[f] = misfit_row[...]
    await_bytes(misfit_rows.at[pl.ds(0, NF - 1)], recv.at[3])
    members = misfit_row.shape[1]
    final_row[:, pl.ds(members, members)] = jnp.sum(misfit_rows[...], axis=0)
    await_bytes(square_rows.at[pl.ds(0, NF - 1)], recv.at[5])
    final_row[:, pl.ds(0, members)] = jnp.sum(square_rows[...], axis=0)
    for i in range(1, NT):
        put(final_row, final_rows.at[tile], send.at[6], recv.at[6], other_tile(i))
    final_rows[tile] = final_row[...]
    await_bytes(final_rows.at[pl.ds(0, NT - 1)], recv.at[6])
    final = jnp.sum(final_rows[...], axis=0)
    misfit = final[:, members:] / (2.0 * total)
    scale = jnp.sqrt(final[:, :members] / ncells + EPSILON)
    out_ref[...] = models_ref[...] - STEP_LENGTH * (misfit / scale) * gradient
    misfit_ref[...] = misfit

    for c in range(chunks):
        await_bytes(buf.at[c, pl.ds(0, NF - 1)], bulk_send.at[c])
    await_bytes(tiles.at[pl.ds(0, NT - 1)], send.at[0])
    await_bytes(gathered.at[0, pl.ds(0, NZ - 1)], send.at[1])
    await_bytes(gathered.at[pl.ds(0, NX - 1)], send.at[2])
    await_bytes(misfit_rows.at[pl.ds(0, NF - 1)], send.at[3])
    await_bytes(trecv.at[pl.ds(0, NT - 1)], send.at[4])
    await_bytes(square_rows.at[pl.ds(0, NF - 1)], send.at[5])
    await_bytes(final_rows.at[pl.ds(0, NT - 1)], send.at[6])
    for b in range(2):
        await_bytes(xrecv.at[b, pl.ds(0, NX - 1)], pair_send.at[0, b])
        await_bytes(zrecv.at[b, pl.ds(0, NZ - 1)], pair_send.at[1, b])


def body(sensitivity, models, observed, waveform, cell_index, gate_index):
    owned, members = models.shape
    gates = gate_index.shape[0]
    ncell = cell_index.shape[1]
    chunks = sensitivity.shape[3] // NF // ROWS
    table = jnp.asarray(kernel_table(NF, waveform.shape[0]))
    vmem, smem = pl.BlockSpec(memory_space=pltpu.VMEM), pl.BlockSpec(memory_space=pltpu.SMEM)
    dma = pltpu.SemaphoreType.DMA
    updated, misfit = pl.pallas_call(
        kernel,
        out_shape=(jax.ShapeDtypeStruct((owned, members), F32), jax.ShapeDtypeStruct((1, members), F32)),
        in_specs=[smem, smem, pl.BlockSpec(memory_space=pl.ANY), vmem, vmem, vmem, vmem],
        out_specs=(vmem, vmem),
        scratch_shapes=[
            pltpu.VMEM((chunks, NF, 2, ROWS, ncell), F32),
            pltpu.VMEM((NT, ROWS, members), F32),
            pltpu.VMEM((NX, NZ, 2, ROWS, members), F32),
            pltpu.VMEM((2, gates * ROWS, 2 * NF * ROWS), BF16),
            pltpu.VMEM((gates * ROWS, chunks * ROWS), F32),
            pltpu.VMEM((ncell, ncell), BF16),
            pltpu.VMEM((2, members, ncell), BF16),
            pltpu.VMEM((members, ncell), F32),
            pltpu.VMEM((2, NX, NZ, ROWS, members), F32),
            pltpu.VMEM((2, NX, NZ, ROWS, members), F32),
            pltpu.VMEM((2, NZ, ROWS, members), F32),
            pltpu.VMEM((2, NZ, ROWS, members), F32),
            pltpu.VMEM((NT, ROWS, members), F32),
            pltpu.VMEM((NT, ROWS, members), F32),
            pltpu.VMEM((1, members), F32),
            pltpu.VMEM((NF, 1, members), F32),
            pltpu.VMEM((1, members), F32),
            pltpu.VMEM((NF, 1, members), F32),
            pltpu.VMEM((1, 2 * members), F32),
            pltpu.VMEM((NT, 1, 2 * members), F32),
            dma((chunks,)), dma((chunks,)), dma((7,)), dma((7,)), dma((2, 2)), dma((2, 2)),
        ],
        compiler_params=pltpu.CompilerParams(collective_id=0, has_side_effects=True, vmem_limit_bytes=60 << 20),
    )(waveform, gate_index, sensitivity, models, observed, cell_index, table)
    return updated, misfit[0]


def solution(mesh):
    in_specs = (
        P("tile", "freq", None, None, None),
        P(("tile", "freq"), None),
        P("tile", None, "freq"),
        P(),
        P("tile", None),
        P(),
    )
    out_specs = (P(("tile", "freq"), None), P())
    return jax.shard_map(body, mesh=mesh, in_specs=in_specs, out_specs=out_specs, check_vma=False)
```

```python
import functools
import math

import jax
import jax.numpy as jnp
import numpy as np
from jax import lax
from jax.experimental import pallas as pl
from jax.experimental.pallas import tpu as pltpu
from jax.sharding import PartitionSpec as P

HIGH = lax.Precision.HIGHEST
PHASE_RATE = 0.37
STEP_LENGTH = 0.5
EPSILON = 1e-06
MESH = pl.DeviceIdType.MESH
NX, NZ, NT = 4, 8, 8
NF = NX * NZ
ROWS = 8
F32, BF16 = jnp.float32, jnp.bfloat16


def kernel_table(freqs, samples):
    freq_col = np.arange(freqs, dtype=np.float32)[:, None] + np.float32(0.5)
    time_row = np.arange(samples, dtype=np.float32)[None, :] + np.float32(0.5)
    phases = ((np.float32(PHASE_RATE) * freq_col) * time_row).astype(np.float64)
    table = np.stack([np.cos(phases), np.sin(phases)], axis=1) / math.sqrt(freqs)
    return table.reshape(2 * freqs, samples).astype(np.float32)


def nn(a, b, precision=None):
    return lax.dot_general(a, b, (((1,), (0,)), ((), ())), precision=precision, preferred_element_type=F32)


def nt(a, b, precision=None):
    return lax.dot_general(a, b, (((1,), (1,)), ((), ())), precision=precision, preferred_element_type=F32)


def split(a):
    high = a.astype(BF16)
    return high, (a - high.astype(F32)).astype(BF16)


def three(dot, a, b):
    return dot(a[0], b[0]) + dot(a[0], b[1]) + dot(a[1], b[0])


def iota(shape, dim):
    return lax.broadcasted_iota(jnp.int32, shape, dim)


def await_bytes(ref, sem):
    pltpu.make_async_copy(ref, ref, sem).wait()


def kernel(
    wave_in, gate_in, sens_ref, models_in, obs_in, cell_in, table_in,
    gradient_ref, final_ref,
    wave_ref, gate_ref, models_ref, obs_ref, cell_ref, table_ref,
    buf, tiles, gathered, wide, expanded, onehot, model_t, cells_t, grads, xrecv, zsend, zrecv, tsend, trecv,
    square_row, square_rows, misfit_row, misfit_rows, final_row, final_rows,
    bulk_send, bulk_recv, send, recv, pair_send, pair_recv, load,
):
    tile = lax.axis_index("tile")
    f = lax.axis_index("freq")
    x, z = f // NZ, lax.rem(f, NZ)
    chunks = buf.shape[0]
    soundings = chunks * ROWS
    gates = obs_ref.shape[1]

    def plane(i):
        return {"freq": lax.rem(x + i // NZ, NX) * NZ + lax.rem(z + i % NZ, NZ)}

    def other_tile(i):
        return {"tile": lax.rem(tile + i, NT)}

    def put(src, dst, send_sem, recv_sem, device):
        pltpu.make_async_remote_copy(
            src_ref=src, dst_ref=dst, send_sem=send_sem, recv_sem=recv_sem, device_id=device, device_id_type=MESH
        ).start()

    loads = [
        pltpu.make_async_copy(src, dst, load.at[i])
        for i, (src, dst) in enumerate((
            (models_in, models_ref), (cell_in, cell_ref), (gate_in, gate_ref),
            (wave_in, wave_ref), (table_in, table_ref), (obs_in.at[0], obs_ref),
        ))
    ]
    for copy in loads:
        copy.start()
    barrier = pltpu.get_barrier_semaphore()
    for i in range(1, NF):
        pl.semaphore_signal(barrier, inc=1, device_id=plane(i), device_id_type=MESH)
    for i in range(1, NT):
        pl.semaphore_signal(barrier, inc=1, device_id=other_tile(i), device_id_type=MESH)
    loads[0].wait()
    pl.semaphore_wait(barrier, NF + NT - 2)

    for i in range(1, NT):
        put(models_ref, tiles.at[tile], send.at[0], recv.at[0], other_tile(i))

    def send_chunk(c):
        for i in range(1, NF):
            p = plane(i)
            start = pl.multiple_of(p["freq"] * soundings + c * ROWS, ROWS)
            put(sens_ref.at[0, 0, :, pl.ds(start, ROWS), :], buf.at[c, f], bulk_send.at[c], bulk_recv.at[c], p)
        start = pl.multiple_of(f * soundings + c * ROWS, ROWS)
        pltpu.make_async_copy(sens_ref.at[0, 0, :, pl.ds(start, ROWS), :], buf.at[c, f], bulk_recv.at[c]).start()

    send_chunk(0)

    for copy in loads[1:]:
        copy.wait()
    cells = cell_ref[...]
    block = lax.shift_right_logical(cells, 8)
    partner = jnp.max(jnp.where(block != tile, block, -1), axis=1, keepdims=True)
    local = jnp.where(block == tile, cells & 255, 256 + (cells & 255))
    ncell = cells.shape[1]
    onehot[...] = jnp.where(iota((ncell, ncell), 0) == local, 1.0, 0.0).astype(BF16)

    tiles[tile] = models_ref[...]
    await_bytes(tiles.at[pl.ds(0, NT - 1)], recv.at[0])
    borrowed = jnp.zeros_like(models_ref)
    for t in range(NT):
        borrowed = jnp.where(partner == t, tiles[t], borrowed)
    gathered[x, z, 0] = models_ref[...]
    gathered[x, z, 1] = borrowed
    for i in range(1, NZ):
        put(gathered.at[x, z], gathered.at[x, z], send.at[1], recv.at[1], plane(i))
    send_chunk(1)

    samples = table_ref.shape[1]
    rows = iota((gates, samples), 0)
    lag = lax.fori_loop(0, gates, lambda g, a: jnp.where(rows == g, gate_ref[g], a), jnp.zeros((gates, samples), jnp.int32))
    lag = lag - iota((gates, samples), 1)
    toeplitz = lax.fori_loop(
        0, samples, lambda k, a: jnp.where(lag == k, wave_ref[k], a), jnp.zeros((gates, samples), F32)
    )
    narrow = nt(toeplitz, table_ref[...], HIGH)
    spread = jnp.where(lax.shift_right_logical(iota((gates * ROWS, gates), 0), 3) == iota((gates * ROWS, gates), 1), 1.0, 0.0)
    fps = narrow.shape[1]
    pick = jnp.where(iota((fps, fps * ROWS), 0) == lax.shift_right_logical(iota((fps, fps * ROWS), 1), 3), 1.0, 0.0)
    big = nn(nn(spread, narrow, HIGH), pick, HIGH)
    same = (iota(big.shape, 0) & 7) == (iota(big.shape, 1) & 7)
    big_high, big_low = split(jnp.where(same, big, 0.0))
    wide[0] = big_high
    wide[1] = big_low
    expanded[...] = nt(spread, obs_ref[...], HIGH)

    await_bytes(gathered.at[0, pl.ds(0, NZ - 1)], recv.at[1])
    for i in range(1, NX):
        put(gathered.at[x], gathered.at[x], send.at[2], recv.at[2], plane(i * NZ))
    send_chunk(2)
    send_chunk(3)

    await_bytes(gathered.at[pl.ds(0, NX - 1)], recv.at[2])
    for b in range(2):
        part = gathered[:, :, b].reshape(NF * ROWS, -1)
        part_high, part_low = split(part.T)
        hot = onehot[pl.ds(b * NF * ROWS, NF * ROWS), :]
        if b == 0:
            model_high, model_low = nn(part_high, hot), nn(part_low, hot)
        else:
            model_high, model_low = model_high + nn(part_high, hot), model_low + nn(part_low, hot)
    model_t[0] = model_high.astype(BF16)
    model_t[1] = model_low.astype(BF16)

    cells_t[...] = jnp.zeros_like(cells_t)
    misfit_row[...] = jnp.zeros_like(misfit_row)

    def chunk(c, carry):
        await_bytes(buf.at[c], bulk_recv.at[c])
        block_s = split(buf[c].reshape(fps * ROWS, ncell))
        operator = split(three(nn, (wide[0], wide[1]), block_s))
        seen = expanded[...]
        seen = jnp.where(iota(seen.shape, 1) == c * ROWS + (iota(seen.shape, 0) & 7), seen, 0.0)
        seen_row = nt(jnp.ones((8, seen.shape[1]), F32), seen, HIGH)[0:1]
        rows_t = three(nt, (model_t[0], model_t[1]), operator) - seen_row
        misfit_row[...] += nt(jnp.ones((8, rows_t.shape[1]), F32), rows_t * rows_t, HIGH)[0:1]
        cells_t[...] += three(nn, split(rows_t), operator)
        return carry

    lax.fori_loop(0, chunks, chunk, 0)

    grad_high, grad_low = split(cells_t[...])
    half = NF * ROWS
    for b in (1, 0):
        hot = onehot[pl.ds(b * half, half), :]
        part = nt(hot, grad_high) + nt(hot, grad_low)
        grads[b] = part.reshape(NX, NZ, ROWS, -1)
        if b == 0:
            await_bytes(xrecv.at[1, pl.ds(0, NX - 1)], pair_send.at[0, 1])
        for i in range(1, NX):
            p = lax.rem(x + i, NX)
            put(grads.at[b, p], xrecv.at[b, x], pair_send.at[0, b], pair_recv.at[0, b], plane(i * NZ))
    for i in range(1, NF):
        put(misfit_row, misfit_rows.at[f], send.at[3], recv.at[3], plane(i))
    for b in (1, 0):
        xrecv[b, x] = grads[b, x]
        await_bytes(xrecv.at[b, pl.ds(0, NX - 1)], pair_recv.at[0, b])
        zsend[b] = (xrecv[b, 0] + xrecv[b, 1]) + (xrecv[b, 2] + xrecv[b, 3])
        for i in range(1, NZ):
            p = lax.rem(z + i, NZ)
            put(zsend.at[b, p], zrecv.at[b, z], pair_send.at[1, b], pair_recv.at[1, b], plane(i))
    sums = []
    for b in (1, 0):
        zrecv[b, z] = zsend[b, z]
        await_bytes(zrecv.at[b, pl.ds(0, NZ - 1)], pair_recv.at[1, b])
        sums.append(jnp.sum(zrecv[b], axis=0))
        if b == 1:
            for t in range(NT):
                tsend[t] = jnp.where(partner == t, sums[0], 0.0)
            for i in range(1, NT):
                put(tsend.at[lax.rem(tile + i, NT)], trecv.at[tile], send.at[4], recv.at[4], other_tile(i))
    trecv[tile] = jnp.zeros_like(sums[0])
    await_bytes(trecv.at[pl.ds(0, NT - 1)], recv.at[4])
    gradient = sums[1] + jnp.sum(trecv[...], axis=0)

    square_row[...] = jnp.sum(gradient * gradient, axis=0, keepdims=True)
    for i in range(1, NF):
        put(square_row, square_rows.at[f], send.at[5], recv.at[5], plane(i))
    square_rows[f] = square_row[...]
    misfit_rows[f] = misfit_row[...]
    await_bytes(misfit_rows.at[pl.ds(0, NF - 1)], recv.at[3])
    members = misfit_row.shape[1]
    final_row[:, pl.ds(members, members)] = jnp.sum(misfit_rows[...], axis=0)
    await_bytes(square_rows.at[pl.ds(0, NF - 1)], recv.at[5])
    final_row[:, pl.ds(0, members)] = jnp.sum(square_rows[...], axis=0)
    for i in range(1, NT):
        put(final_row, final_rows.at[tile], send.at[6], recv.at[6], other_tile(i))
    final_rows[tile] = final_row[...]
    await_bytes(final_rows.at[pl.ds(0, NT - 1)], recv.at[6])
    gradient_ref[...] = gradient
    final_ref[...] = jnp.sum(final_rows[...], axis=0)

    for c in range(chunks):
        await_bytes(buf.at[c, pl.ds(0, NF - 1)], bulk_send.at[c])
    await_bytes(tiles.at[pl.ds(0, NT - 1)], send.at[0])
    await_bytes(gathered.at[0, pl.ds(0, NZ - 1)], send.at[1])
    await_bytes(gathered.at[pl.ds(0, NX - 1)], send.at[2])
    await_bytes(misfit_rows.at[pl.ds(0, NF - 1)], send.at[3])
    await_bytes(trecv.at[pl.ds(0, NT - 1)], send.at[4])
    await_bytes(square_rows.at[pl.ds(0, NF - 1)], send.at[5])
    await_bytes(final_rows.at[pl.ds(0, NT - 1)], send.at[6])
    for b in range(2):
        await_bytes(zrecv.at[b, pl.ds(0, NZ - 1)], pair_send.at[1, b])
    await_bytes(xrecv.at[0, pl.ds(0, NX - 1)], pair_send.at[0, 0])


def finish(total, ncells, models_ref, gradient_ref, final_ref, out_ref, misfit_ref):
    members = models_ref.shape[1]
    misfit = final_ref[:, pl.ds(members, members)] / (2.0 * total)
    scale = jnp.sqrt(final_ref[:, pl.ds(0, members)] / ncells + EPSILON)
    out_ref[...] = models_ref[...] - STEP_LENGTH * (misfit / scale) * gradient_ref[...]
    misfit_ref[...] = misfit


def body(sensitivity, models, observed, waveform, cell_index, gate_index):
    owned, members = models.shape
    gates = gate_index.shape[0]
    ncell = cell_index.shape[1]
    chunks = sensitivity.shape[3] // NF // ROWS
    table = jnp.asarray(kernel_table(NF, waveform.shape[0]))
    hbm, vmem = pl.BlockSpec(memory_space=pl.ANY), pl.BlockSpec(memory_space=pltpu.VMEM)
    dma = pltpu.SemaphoreType.DMA
    gradient, final = pl.pallas_call(
        kernel,
        out_shape=(jax.ShapeDtypeStruct((owned, members), F32), jax.ShapeDtypeStruct((1, 2 * members), F32)),
        in_specs=[hbm] * 7,
        out_specs=(vmem, vmem),
        scratch_shapes=[
            pltpu.SMEM(waveform.shape, F32),
            pltpu.SMEM(gate_index.shape, jnp.int32),
            pltpu.VMEM(models.shape, F32),
            pltpu.VMEM((observed.shape[2], gates), F32),
            pltpu.VMEM(cell_index.shape, jnp.int32),
            pltpu.VMEM(table.shape, F32),
            pltpu.VMEM((chunks, NF, 2, ROWS, ncell), F32),
            pltpu.VMEM((NT, ROWS, members), F32),
            pltpu.VMEM((NX, NZ, 2, ROWS, members), F32),
            pltpu.VMEM((2, gates * ROWS, 2 * NF * ROWS), BF16),
            pltpu.VMEM((gates * ROWS, chunks * ROWS), F32),
            pltpu.VMEM((ncell, ncell), BF16),
            pltpu.VMEM((2, members, ncell), BF16),
            pltpu.VMEM((members, ncell), F32),
            pltpu.VMEM((2, NX, NZ, ROWS, members), F32),
            pltpu.VMEM((2, NX, NZ, ROWS, members), F32),
            pltpu.VMEM((2, NZ, ROWS, members), F32),
            pltpu.VMEM((2, NZ, ROWS, members), F32),
            pltpu.VMEM((NT, ROWS, members), F32),
            pltpu.VMEM((NT, ROWS, members), F32),
            pltpu.VMEM((1, members), F32),
            pltpu.VMEM((NF, 1, members), F32),
            pltpu.VMEM((1, members), F32),
            pltpu.VMEM((NF, 1, members), F32),
            pltpu.VMEM((1, 2 * members), F32),
            pltpu.VMEM((NT, 1, 2 * members), F32),
            dma((chunks,)), dma((chunks,)), dma((7,)), dma((7,)), dma((2, 2)), dma((2, 2)), dma((6,)),
        ],
        compiler_params=pltpu.CompilerParams(collective_id=0, has_side_effects=True, vmem_limit_bytes=60 << 20),
    )(waveform, gate_index, sensitivity, models, jnp.swapaxes(observed, 1, 2), cell_index, table)
    devices = NT * NF
    updated, misfit = pl.pallas_call(
        functools.partial(finish, NT * sensitivity.shape[3] * gates, owned * devices),
        out_shape=(jax.ShapeDtypeStruct((owned, members), F32), jax.ShapeDtypeStruct((1, members), F32)),
        in_specs=[vmem] * 3,
        out_specs=(vmem, vmem),
    )(models, gradient, final)
    return updated, misfit[0]


def solution(mesh):
    in_specs = (
        P("tile", "freq", None, None, None),
        P(("tile", "freq"), None),
        P("tile", None, "freq"),
        P(),
        P("tile", None),
        P(),
    )
    out_specs = (P(("tile", "freq"), None), P())
    return jax.shard_map(body, mesh=mesh, in_specs=in_specs, out_specs=out_specs, check_vma=False)
```

```python
import functools
import math

import jax
import jax.numpy as jnp
import numpy as np
from jax import lax
from jax.experimental import pallas as pl
from jax.experimental.pallas import tpu as pltpu
from jax.sharding import PartitionSpec as P

HIGH = lax.Precision.HIGHEST
PHASE_RATE = 0.37
STEP_LENGTH = 0.5
EPSILON = 1e-06
MESH = pl.DeviceIdType.MESH
NX, NZ, NT = 4, 8, 8
NF = NX * NZ
ROWS = 8
F32, BF16 = jnp.float32, jnp.bfloat16
NEAR_Z, FAR_Z, ALONG_X = [1, 2, NZ - 2, NZ - 1], [3, 4, 5], [NZ, 2 * NZ, 3 * NZ]


def kernel_table(freqs, samples):
    freq_col = np.arange(freqs, dtype=np.float32)[:, None] + np.float32(0.5)
    time_row = np.arange(samples, dtype=np.float32)[None, :] + np.float32(0.5)
    phases = ((np.float32(PHASE_RATE) * freq_col) * time_row).astype(np.float64)
    table = np.stack([np.cos(phases), np.sin(phases)], axis=1) / math.sqrt(freqs)
    return table.reshape(2 * freqs, samples).astype(np.float32)


def nn(a, b, precision=None):
    return lax.dot_general(a, b, (((1,), (0,)), ((), ())), precision=precision, preferred_element_type=F32)


def nt(a, b, precision=None):
    return lax.dot_general(a, b, (((1,), (1,)), ((), ())), precision=precision, preferred_element_type=F32)


def split(a):
    high = a.astype(BF16)
    return high, (a - high.astype(F32)).astype(BF16)


def three(dot, a, b):
    return dot(a[0], b[0]) + dot(a[0], b[1]) + dot(a[1], b[0])


def iota(shape, dim):
    return lax.broadcasted_iota(jnp.int32, shape, dim)


def await_bytes(ref, sem):
    pltpu.make_async_copy(ref, ref, sem).wait()


def kernel(
    wave_in, gate_in, sens_ref, models_in, obs_in, cell_in, table_in,
    gradient_ref, final_ref,
    wave_ref, gate_ref, models_ref, obs_ref, cell_ref, table_ref,
    buf, tiles, gathered, wide, expanded, onehot, model_t, cells_t, lent, lent_x, lent_sum, lent_z, own, own_z, own_sum, own_x,
    shared, partner_row, partners,
    square_row, square_rows, misfit_row, misfit_tiles, misfit_sum, misfit_rows,
    bulk_send, bulk_recv, send, recv, pair_send, pair_recv, load, known,
):
    tile = lax.axis_index("tile")
    f = lax.axis_index("freq")
    x, z = f // NZ, lax.rem(f, NZ)
    chunks = buf.shape[0]
    soundings = chunks * ROWS
    gates = obs_ref.shape[1]

    def plane(i):
        return {"freq": lax.rem(x + i // NZ, NX) * NZ + lax.rem(z + i % NZ, NZ)}

    def other_tile(i):
        return {"tile": lax.rem(tile + i, NT)}

    def put(src, dst, send_sem, recv_sem, device):
        pltpu.make_async_remote_copy(
            src_ref=src, dst_ref=dst, send_sem=send_sem, recv_sem=recv_sem, device_id=device, device_id_type=MESH
        ).start()

    loads = [
        pltpu.make_async_copy(src, dst, load.at[i])
        for i, (src, dst) in enumerate((
            (models_in, models_ref), (cell_in, cell_ref), (gate_in, gate_ref),
            (wave_in, wave_ref), (table_in, table_ref), (obs_in.at[0], obs_ref),
        ))
    ]
    for copy in loads:
        copy.start()
    barrier = pltpu.get_barrier_semaphore()
    for i in NEAR_Z + ALONG_X:
        pl.semaphore_signal(barrier, inc=1, device_id=plane(i), device_id_type=MESH)
    for i in range(1, NT):
        pl.semaphore_signal(barrier, inc=1, device_id=other_tile(i), device_id_type=MESH)
    loads[0].wait()
    pl.semaphore_wait(barrier, len(NEAR_Z + ALONG_X) + NT - 1)

    for i in range(1, NT):
        put(models_ref, tiles.at[tile], send.at[0], recv.at[0], other_tile(i))

    def send_chunk(c, peers=range(1, NF)):
        for i in peers:
            p = plane(i)
            start = pl.multiple_of(p["freq"] * soundings + c * ROWS, ROWS)
            put(sens_ref.at[0, 0, :, pl.ds(start, ROWS), :], buf.at[c, f], bulk_send.at[c], bulk_recv.at[c], p)

    def keep_chunk(c):
        start = pl.multiple_of(f * soundings + c * ROWS, ROWS)
        pltpu.make_async_copy(sens_ref.at[0, 0, :, pl.ds(start, ROWS), :], buf.at[c, f], bulk_recv.at[c]).start()

    send_chunk(0, NEAR_Z + ALONG_X)
    for i in (2, NZ - 2):
        pl.semaphore_signal(known.at[0], inc=1, device_id=plane(i), device_id_type=MESH)
    pl.semaphore_wait(known.at[0], 2)
    for i in ALONG_X:
        pl.semaphore_signal(known.at[1], inc=1, device_id=plane(i), device_id_type=MESH)
    send_chunk(0, FAR_Z)
    pl.semaphore_wait(known.at[1], len(ALONG_X))
    send_chunk(0, [i for i in range(1, NF) if i not in NEAR_Z + ALONG_X + FAR_Z])
    for c in range(chunks):
        keep_chunk(c)

    for copy in loads[1:]:
        copy.wait()
    cells = cell_ref[...]
    block = lax.shift_right_logical(cells, 8)
    partner = jnp.max(jnp.where(block != tile, block, -1), axis=1, keepdims=True)
    local = jnp.where(block == tile, cells & 255, 256 + (cells & 255))
    ncell = cells.shape[1]
    onehot[...] = jnp.where(iota((ncell, ncell), 0) == local, 1.0, 0.0).astype(BF16)

    partner_row[...] = jnp.broadcast_to(partner.astype(F32), partner_row.shape)
    for i in range(1, NT):
        put(partner_row, partners.at[tile], send.at[6], recv.at[6], other_tile(i))
    partners[tile] = partner_row[...]
    tiles[tile] = models_ref[...]
    await_bytes(tiles.at[pl.ds(0, NT - 1)], recv.at[0])
    borrowed = jnp.zeros_like(models_ref)
    for t in range(NT):
        borrowed = jnp.where(partner == t, tiles[t], borrowed)
    gathered[x, z, 0] = models_ref[...]
    gathered[x, z, 1] = borrowed
    for i in range(1, NZ):
        put(gathered.at[x, z], gathered.at[x, z], send.at[1], recv.at[1], plane(i))
    send_chunk(1)

    samples = table_ref.shape[1]
    rows = iota((gates, samples), 0)
    lag = lax.fori_loop(0, gates, lambda g, a: jnp.where(rows == g, gate_ref[g], a), jnp.zeros((gates, samples), jnp.int32))
    lag = lag - iota((gates, samples), 1)
    toeplitz = lax.fori_loop(
        0, samples, lambda k, a: jnp.where(lag == k, wave_ref[k], a), jnp.zeros((gates, samples), F32)
    )
    narrow = nt(toeplitz, table_ref[...], HIGH)
    spread = jnp.where(lax.shift_right_logical(iota((gates * ROWS, gates), 0), 3) == iota((gates * ROWS, gates), 1), 1.0, 0.0)
    fps = narrow.shape[1]
    pick = jnp.where(iota((fps, fps * ROWS), 0) == lax.shift_right_logical(iota((fps, fps * ROWS), 1), 3), 1.0, 0.0)
    big = nn(nn(spread, narrow, HIGH), pick, HIGH)
    same = (iota(big.shape, 0) & 7) == (iota(big.shape, 1) & 7)
    big_high, big_low = split(jnp.where(same, big, 0.0))
    wide[0] = big_high
    wide[1] = big_low
    expanded[...] = nt(spread, obs_ref[...], HIGH)

    await_bytes(gathered.at[0, pl.ds(0, NZ - 1)], recv.at[1])
    for i in range(1, NX):
        put(gathered.at[x], gathered.at[x], send.at[2], recv.at[2], plane(i * NZ))
    send_chunk(2)
    send_chunk(3)

    await_bytes(gathered.at[pl.ds(0, NX - 1)], recv.at[2])
    for b in range(2):
        part = gathered[:, :, b].reshape(NF * ROWS, -1)
        part_high, part_low = split(part.T)
        hot = onehot[pl.ds(b * NF * ROWS, NF * ROWS), :]
        if b == 0:
            model_high, model_low = nn(part_high, hot), nn(part_low, hot)
        else:
            model_high, model_low = model_high + nn(part_high, hot), model_low + nn(part_low, hot)
    model_t[0] = model_high.astype(BF16)
    model_t[1] = model_low.astype(BF16)

    cells_t[...] = jnp.zeros_like(cells_t)
    misfit_row[...] = jnp.zeros_like(misfit_row)

    def chunk(c, carry):
        await_bytes(buf.at[c], bulk_recv.at[c])
        block_s = split(buf[c].reshape(fps * ROWS, ncell))
        operator = split(three(nn, (wide[0], wide[1]), block_s))
        seen = expanded[...]
        seen = jnp.where(iota(seen.shape, 1) == c * ROWS + (iota(seen.shape, 0) & 7), seen, 0.0)
        seen_row = nt(jnp.ones((8, seen.shape[1]), F32), seen, HIGH)[0:1]
        rows_t = three(nt, (model_t[0], model_t[1]), operator) - seen_row
        misfit_row[...] += nt(jnp.ones((8, rows_t.shape[1]), F32), rows_t * rows_t, HIGH)[0:1]
        cells_t[...] += three(nn, split(rows_t), operator)
        return carry

    lax.fori_loop(0, chunks, chunk, 0)

    grad_high, grad_low = split(cells_t[...])
    half = NF * ROWS

    def global_rows(b):
        hot = onehot[pl.ds(b * half, half), :]
        return (nt(hot, grad_high) + nt(hot, grad_low)).reshape(NX, NZ, ROWS, -1)

    lent[...] = global_rows(1)
    for i in range(1, NX):
        p = lax.rem(x + i, NX)
        put(lent.at[p], lent_x.at[x], pair_send.at[0], pair_recv.at[0], plane(i * NZ))
    own[...] = jnp.swapaxes(global_rows(0), 0, 1)
    for i in range(1, NZ):
        p = lax.rem(z + i, NZ)
        put(own.at[p], own_z.at[z], pair_send.at[1], pair_recv.at[1], plane(i))
    for i in range(1, NT):
        put(misfit_row, misfit_tiles.at[tile], send.at[7], recv.at[7], other_tile(i))

    lent_x[x] = lent[x]
    await_bytes(lent_x.at[pl.ds(0, NX - 1)], pair_recv.at[0])
    lent_sum[...] = (lent_x[0] + lent_x[1]) + (lent_x[2] + lent_x[3])
    for i in range(1, NZ):
        p = lax.rem(z + i, NZ)
        put(lent_sum.at[p], lent_z.at[z], pair_send.at[2], pair_recv.at[2], plane(i))
    own_z[z] = own[z]
    await_bytes(own_z.at[pl.ds(0, NZ - 1)], pair_recv.at[1])
    own_sum[...] = jnp.sum(own_z[...], axis=0)
    for i in range(1, NX):
        p = lax.rem(x + i, NX)
        put(own_sum.at[p], own_x.at[x], pair_send.at[3], pair_recv.at[3], plane(i * NZ))
    lent_z[z] = lent_sum[z]
    await_bytes(lent_z.at[pl.ds(0, NZ - 1)], pair_recv.at[2])
    shared[tile, 1] = jnp.sum(lent_z[...], axis=0)
    for i in range(1, NT):
        put(shared.at[tile, 1], shared.at[tile, 1], send.at[4], recv.at[4], other_tile(i))
    own_x[x] = own_sum[x]
    await_bytes(own_x.at[pl.ds(0, NX - 1)], pair_recv.at[3])
    shared[tile, 0] = (own_x[0] + own_x[1]) + (own_x[2] + own_x[3])
    for i in range(1, NT):
        put(shared.at[tile, 0], shared.at[tile, 0], send.at[8], recv.at[8], other_tile(i))
    misfit_tiles[tile] = misfit_row[...]
    await_bytes(misfit_tiles.at[pl.ds(0, NT - 1)], recv.at[7])
    misfit_sum[...] = jnp.sum(misfit_tiles[...], axis=0)
    for i in range(1, NF):
        put(misfit_sum, misfit_rows.at[f], send.at[3], recv.at[3], plane(i))
    await_bytes(partners.at[pl.ds(0, NT - 1)], recv.at[6])
    await_bytes(shared.at[pl.ds(0, NT - 1), 1], recv.at[4])
    await_bytes(shared.at[pl.ds(0, NT - 1), 0], recv.at[8])

    def gradient_of(t, own_rows):
        for lender in range(NT):
            own_rows = own_rows + jnp.where(partners[lender][:, 0:1] == t, shared[lender, 1], 0.0)
        return own_rows

    squares = jnp.zeros_like(models_ref)
    for t in range(NT):
        rows_of = gradient_of(float(t), shared[t, 0])
        squares = squares + rows_of * rows_of
    square_row[...] = jnp.sum(squares, axis=0, keepdims=True)
    for i in range(1, NF):
        put(square_row, square_rows.at[f], send.at[5], recv.at[5], plane(i))
    gradient_ref[...] = gradient_of(tile.astype(F32), shared[tile, 0])
    square_rows[f] = square_row[...]
    misfit_rows[f] = misfit_sum[...]
    await_bytes(misfit_rows.at[pl.ds(0, NF - 1)], recv.at[3])
    members = misfit_row.shape[1]
    final_ref[:, pl.ds(members, members)] = jnp.sum(misfit_rows[...], axis=0)
    await_bytes(square_rows.at[pl.ds(0, NF - 1)], recv.at[5])
    final_ref[:, pl.ds(0, members)] = jnp.sum(square_rows[...], axis=0)

    for c in range(chunks):
        await_bytes(buf.at[c, pl.ds(0, NF - 1)], bulk_send.at[c])
    await_bytes(tiles.at[pl.ds(0, NT - 1)], send.at[0])
    await_bytes(gathered.at[0, pl.ds(0, NZ - 1)], send.at[1])
    await_bytes(gathered.at[pl.ds(0, NX - 1)], send.at[2])
    await_bytes(misfit_rows.at[pl.ds(0, NF - 1)], send.at[3])
    await_bytes(shared.at[pl.ds(0, NT - 1), 1], send.at[4])
    await_bytes(shared.at[pl.ds(0, NT - 1), 0], send.at[8])
    await_bytes(misfit_tiles.at[pl.ds(0, NT - 1)], send.at[7])
    await_bytes(square_rows.at[pl.ds(0, NF - 1)], send.at[5])
    await_bytes(partners.at[pl.ds(0, NT - 1)], send.at[6])
    await_bytes(lent_x.at[pl.ds(0, NX - 1)], pair_send.at[0])
    await_bytes(own_z.at[pl.ds(0, NZ - 1)], pair_send.at[1])
    await_bytes(lent_z.at[pl.ds(0, NZ - 1)], pair_send.at[2])
    await_bytes(own_x.at[pl.ds(0, NX - 1)], pair_send.at[3])


def finish(total, ncells, models_ref, gradient_ref, final_ref, out_ref, misfit_ref):
    members = models_ref.shape[1]
    misfit = final_ref[:, pl.ds(members, members)] / (2.0 * total)
    scale = jnp.sqrt(final_ref[:, pl.ds(0, members)] / ncells + EPSILON)
    out_ref[...] = models_ref[...] - STEP_LENGTH * (misfit / scale) * gradient_ref[...]
    misfit_ref[...] = misfit


def body(sensitivity, models, observed, waveform, cell_index, gate_index):
    owned, members = models.shape
    gates = gate_index.shape[0]
    ncell = cell_index.shape[1]
    chunks = sensitivity.shape[3] // NF // ROWS
    table = jnp.asarray(kernel_table(NF, waveform.shape[0]))
    hbm, vmem = pl.BlockSpec(memory_space=pl.ANY), pl.BlockSpec(memory_space=pltpu.VMEM)
    dma = pltpu.SemaphoreType.DMA
    gradient, final = pl.pallas_call(
        kernel,
        out_shape=(jax.ShapeDtypeStruct((owned, members), F32), jax.ShapeDtypeStruct((1, 2 * members), F32)),
        in_specs=[hbm] * 7,
        out_specs=(vmem, vmem),
        scratch_shapes=[
            pltpu.SMEM(waveform.shape, F32),
            pltpu.SMEM(gate_index.shape, jnp.int32),
            pltpu.VMEM(models.shape, F32),
            pltpu.VMEM((observed.shape[2], gates), F32),
            pltpu.VMEM(cell_index.shape, jnp.int32),
            pltpu.VMEM(table.shape, F32),
            pltpu.VMEM((chunks, NF, 2, ROWS, ncell), F32),
            pltpu.VMEM((NT, ROWS, members), F32),
            pltpu.VMEM((NX, NZ, 2, ROWS, members), F32),
            pltpu.VMEM((2, gates * ROWS, 2 * NF * ROWS), BF16),
            pltpu.VMEM((gates * ROWS, chunks * ROWS), F32),
            pltpu.VMEM((ncell, ncell), BF16),
            pltpu.VMEM((2, members, ncell), BF16),
            pltpu.VMEM((members, ncell), F32),
            pltpu.VMEM((NX, NZ, ROWS, members), F32),
            pltpu.VMEM((NX, NZ, ROWS, members), F32),
            pltpu.VMEM((NZ, ROWS, members), F32),
            pltpu.VMEM((NZ, ROWS, members), F32),
            pltpu.VMEM((NZ, NX, ROWS, members), F32),
            pltpu.VMEM((NZ, NX, ROWS, members), F32),
            pltpu.VMEM((NX, ROWS, members), F32),
            pltpu.VMEM((NX, ROWS, members), F32),
            pltpu.VMEM((NT, 2, ROWS, members), F32),
            pltpu.VMEM((1, 128), F32),
            pltpu.VMEM((NT, 1, 128), F32),
            pltpu.VMEM((1, members), F32),
            pltpu.VMEM((NF, 1, members), F32),
            pltpu.VMEM((1, members), F32),
            pltpu.VMEM((NT, 1, members), F32),
            pltpu.VMEM((1, members), F32),
            pltpu.VMEM((NF, 1, members), F32),
            dma((chunks,)), dma((chunks,)), dma((9,)), dma((9,)), dma((4,)), dma((4,)), dma((6,)), pltpu.SemaphoreType.REGULAR((2,)),
        ],
        compiler_params=pltpu.CompilerParams(collective_id=0, has_side_effects=True, vmem_limit_bytes=60 << 20),
    )(waveform, gate_index, sensitivity, models, jnp.swapaxes(observed, 1, 2), cell_index, table)
    devices = NT * NF
    updated, misfit = pl.pallas_call(
        functools.partial(finish, NT * sensitivity.shape[3] * gates, owned * devices),
        out_shape=(jax.ShapeDtypeStruct((owned, members), F32), jax.ShapeDtypeStruct((1, members), F32)),
        in_specs=[vmem] * 3,
        out_specs=(vmem, vmem),
    )(models, gradient, final)
    return updated, misfit[0]


def solution(mesh):
    in_specs = (
        P("tile", "freq", None, None, None),
        P(("tile", "freq"), None),
        P("tile", None, "freq"),
        P(),
        P("tile", None),
        P(),
    )
    out_specs = (P(("tile", "freq"), None), P())
    return jax.shard_map(body, mesh=mesh, in_specs=in_specs, out_specs=out_specs, check_vma=False)
```

```python
import functools
import math

import jax
import jax.numpy as jnp
import numpy as np
from jax import lax
from jax.experimental import pallas as pl
from jax.experimental.pallas import tpu as pltpu
from jax.sharding import PartitionSpec as P

HIGH = lax.Precision.HIGHEST
PHASE_RATE = 0.37
STEP_LENGTH = 0.5
EPSILON = 1e-06
MESH = pl.DeviceIdType.MESH
NX, NZ, NT = 4, 8, 8
NF = NX * NZ
ROWS = 8
F32, BF16 = jnp.float32, jnp.bfloat16
NEAR_Z, FAR_Z, ALONG_X = [1, 2, NZ - 2, NZ - 1], [3, 4, 5], [NZ, 2 * NZ, 3 * NZ]


def kernel_table(freqs, samples):
    freq_col = np.arange(freqs, dtype=np.float32)[:, None] + np.float32(0.5)
    time_row = np.arange(samples, dtype=np.float32)[None, :] + np.float32(0.5)
    phases = ((np.float32(PHASE_RATE) * freq_col) * time_row).astype(np.float64)
    table = np.stack([np.cos(phases), np.sin(phases)], axis=1) / math.sqrt(freqs)
    return table.reshape(2 * freqs, samples).astype(np.float32)


def nn(a, b, precision=None):
    return lax.dot_general(a, b, (((1,), (0,)), ((), ())), precision=precision, preferred_element_type=F32)


def nt(a, b, precision=None):
    return lax.dot_general(a, b, (((1,), (1,)), ((), ())), precision=precision, preferred_element_type=F32)


def split(a):
    high = a.astype(BF16)
    return high, (a - high.astype(F32)).astype(BF16)


def three(dot, a, b):
    return dot(a[0], b[0]) + dot(a[0], b[1]) + dot(a[1], b[0])


def iota(shape, dim):
    return lax.broadcasted_iota(jnp.int32, shape, dim)


def await_bytes(ref, sem):
    pltpu.make_async_copy(ref, ref, sem).wait()


def kernel(
    wave_in, gate_in, sens_ref, models_in, obs_in, cell_in, table_in,
    gradient_ref, final_ref,
    wave_ref, gate_ref, models_ref, obs_ref, cell_ref, table_ref,
    buf, tiles, gathered, wide, expanded, onehot, model_t, rows_ref, cells_t, lent, lent_x, lent_sum, lent_z, own, own_z, own_sum, own_x,
    shared, partner_row, partners,
    square_row, square_rows, misfit_row, misfit_tiles, misfit_sum, misfit_rows,
    bulk_send, bulk_recv, send, recv, pair_send, pair_recv, load, known, ring_send, ring_recv,
):
    tile = lax.axis_index("tile")
    f = lax.axis_index("freq")
    x, z = f // NZ, lax.rem(f, NZ)
    chunks = buf.shape[0]
    soundings = chunks * ROWS
    gates = obs_ref.shape[1]

    def plane(i):
        return {"freq": lax.rem(x + i // NZ, NX) * NZ + lax.rem(z + i % NZ, NZ)}

    def other_tile(i):
        return {"tile": lax.rem(tile + i, NT)}

    def put(src, dst, send_sem, recv_sem, device):
        pltpu.make_async_remote_copy(
            src_ref=src, dst_ref=dst, send_sem=send_sem, recv_sem=recv_sem, device_id=device, device_id_type=MESH
        ).start()

    loads = [
        pltpu.make_async_copy(src, dst, load.at[i])
        for i, (src, dst) in enumerate((
            (models_in, models_ref), (cell_in, cell_ref), (gate_in, gate_ref),
            (wave_in, wave_ref), (table_in, table_ref), (obs_in.at[0], obs_ref),
        ))
    ]
    for copy in loads:
        copy.start()
    barrier = pltpu.get_barrier_semaphore()
    for i in NEAR_Z + ALONG_X:
        pl.semaphore_signal(barrier, inc=1, device_id=plane(i), device_id_type=MESH)
    for i in range(1, NT):
        pl.semaphore_signal(barrier, inc=1, device_id=other_tile(i), device_id_type=MESH)
    loads[0].wait()
    pl.semaphore_wait(barrier, len(NEAR_Z + ALONG_X) + NT - 1)

    for i in range(1, NT):
        put(models_ref, tiles.at[tile], send.at[0], recv.at[0], other_tile(i))

    def send_chunk(c, peers=range(1, NF)):
        for i in peers:
            p = plane(i)
            start = pl.multiple_of(p["freq"] * soundings + c * ROWS, ROWS)
            put(sens_ref.at[0, 0, :, pl.ds(start, ROWS), :], buf.at[c, f], bulk_send.at[c], bulk_recv.at[c], p)

    def keep_chunk(c):
        start = pl.multiple_of(f * soundings + c * ROWS, ROWS)
        pltpu.make_async_copy(sens_ref.at[0, 0, :, pl.ds(start, ROWS), :], buf.at[c, f], bulk_recv.at[c]).start()

    send_chunk(0, NEAR_Z + ALONG_X)
    for i in (2, NZ - 2):
        pl.semaphore_signal(known.at[0], inc=1, device_id=plane(i), device_id_type=MESH)
    pl.semaphore_wait(known.at[0], 2)
    for i in ALONG_X:
        pl.semaphore_signal(known.at[1], inc=1, device_id=plane(i), device_id_type=MESH)
    send_chunk(0, FAR_Z)
    pl.semaphore_wait(known.at[1], len(ALONG_X))
    send_chunk(0, [i for i in range(1, NF) if i not in NEAR_Z + ALONG_X + FAR_Z])
    for c in range(chunks):
        keep_chunk(c)

    for copy in loads[1:]:
        copy.wait()
    cells = cell_ref[...]
    block = lax.shift_right_logical(cells, 8)
    partner = jnp.max(jnp.where(block != tile, block, -1), axis=1, keepdims=True)
    local = jnp.where(block == tile, cells & 255, 256 + (cells & 255))
    ncell = cells.shape[1]
    onehot[...] = jnp.where(iota((ncell, ncell), 0) == local, 1.0, 0.0).astype(BF16)

    partner_row[...] = jnp.broadcast_to(partner.astype(F32), partner_row.shape)
    for i in range(1, NT):
        put(partner_row, partners.at[tile], send.at[6], recv.at[6], other_tile(i))
    partners[tile] = partner_row[...]
    tiles[tile] = models_ref[...]
    await_bytes(tiles.at[pl.ds(0, NT - 1)], recv.at[0])
    borrowed = jnp.zeros_like(models_ref)
    for t in range(NT):
        borrowed = jnp.where(partner == t, tiles[t], borrowed)
    gathered[x, z, 0] = models_ref[...]
    gathered[x, z, 1] = borrowed

    def pass_on(step):
        down, up = lax.rem(z - step + 1 + NZ, NZ), lax.rem(z + step - 1, NZ)
        for to, block_z, part in ((1, down, 0), (NZ - 1, up, 1)):
            block_ref = gathered.at[x, block_z] if 2 * step < NZ else gathered.at[x, block_z, part]
            put(block_ref, block_ref, ring_send.at[step - 1], ring_recv.at[step - 1], plane(to))

    def passed(step, sems):
        await_bytes(gathered.at[0, pl.ds(0, 2)] if 2 * step < NZ else gathered.at[0, 0], sems.at[step - 1])

    pass_on(1)
    first, second = range(1, NF // 2), range(NF // 2, NF)
    send_chunk(1, first)

    samples = table_ref.shape[1]
    rows = iota((gates, samples), 0)
    lag = lax.fori_loop(0, gates, lambda g, a: jnp.where(rows == g, gate_ref[g], a), jnp.zeros((gates, samples), jnp.int32))
    lag = lag - iota((gates, samples), 1)
    toeplitz = lax.fori_loop(
        0, samples, lambda k, a: jnp.where(lag == k, wave_ref[k], a), jnp.zeros((gates, samples), F32)
    )
    narrow = nt(toeplitz, table_ref[...], HIGH)
    spread = jnp.where(lax.shift_right_logical(iota((gates * ROWS, gates), 0), 3) == iota((gates * ROWS, gates), 1), 1.0, 0.0)
    fps = narrow.shape[1]
    pick = jnp.where(iota((fps, fps * ROWS), 0) == lax.shift_right_logical(iota((fps, fps * ROWS), 1), 3), 1.0, 0.0)
    big = nn(nn(spread, narrow, HIGH), pick, HIGH)
    same = (iota(big.shape, 0) & 7) == (iota(big.shape, 1) & 7)
    big_high, big_low = split(jnp.where(same, big, 0.0))
    wide[0] = big_high
    wide[1] = big_low
    expanded[...] = nt(spread, obs_ref[...], HIGH)

    passed(1, ring_recv)
    pass_on(2)
    send_chunk(1, second)
    passed(2, ring_recv)
    pass_on(3)
    send_chunk(2, first)
    passed(3, ring_recv)
    pass_on(4)
    send_chunk(2, second)
    passed(4, ring_recv)
    for i in range(1, NX):
        put(gathered.at[x], gathered.at[x], send.at[2], recv.at[2], plane(i * NZ))
    send_chunk(3)

    await_bytes(gathered.at[pl.ds(0, NX - 1)], recv.at[2])
    for b in range(2):
        part = gathered[:, :, b].reshape(NF * ROWS, -1)
        part_high, part_low = split(part.T)
        hot = onehot[pl.ds(b * NF * ROWS, NF * ROWS), :]
        if b == 0:
            model_high, model_low = nn(part_high, hot), nn(part_low, hot)
        else:
            model_high, model_low = model_high + nn(part_high, hot), model_low + nn(part_low, hot)
    model_t[0] = model_high.astype(BF16)
    model_t[1] = model_low.astype(BF16)

    cells_t[...] = jnp.zeros_like(cells_t)
    misfit_row[...] = jnp.zeros_like(misfit_row)

    rows_ref[...] = jnp.zeros_like(rows_ref)

    def add_squares():
        rows_t = rows_ref[...]
        misfit_row[...] += nt(jnp.ones((8, rows_t.shape[1]), F32), rows_t * rows_t, HIGH)[0:1]

    def chunk(c, carry):
        add_squares()
        seen = expanded[...]
        seen = jnp.where(iota(seen.shape, 1) == c * ROWS + (iota(seen.shape, 0) & 7), seen, 0.0)
        seen_row = nt(jnp.ones((8, seen.shape[1]), F32), seen, HIGH)[0:1]
        await_bytes(buf.at[c], bulk_recv.at[c])
        block_s = split(buf[c].reshape(fps * ROWS, ncell))
        operator = split(three(nn, (wide[0], wide[1]), block_s))
        rows_t = three(nt, (model_t[0], model_t[1]), operator) - seen_row
        rows_ref[...] = rows_t
        cells_t[...] += three(nn, split(rows_t), operator)
        return carry

    lax.fori_loop(0, chunks, chunk, 0)

    grad_high, grad_low = split(cells_t[...])
    half = NF * ROWS

    def global_rows(b):
        hot = onehot[pl.ds(b * half, half), :]
        return (nt(hot, grad_high) + nt(hot, grad_low)).reshape(NX, NZ, ROWS, -1)

    lent[...] = global_rows(1)
    for i in range(1, NX):
        p = lax.rem(x + i, NX)
        put(lent.at[p], lent_x.at[x], pair_send.at[0], pair_recv.at[0], plane(i * NZ))
    own[...] = jnp.swapaxes(global_rows(0), 0, 1)
    for i in range(1, NZ):
        p = lax.rem(z + i, NZ)
        put(own.at[p], own_z.at[z], pair_send.at[1], pair_recv.at[1], plane(i))
    add_squares()
    for i in range(1, NT):
        put(misfit_row, misfit_tiles.at[tile], send.at[7], recv.at[7], other_tile(i))

    lent_x[x] = lent[x]
    await_bytes(lent_x.at[pl.ds(0, NX - 1)], pair_recv.at[0])
    lent_sum[...] = (lent_x[0] + lent_x[1]) + (lent_x[2] + lent_x[3])
    for i in range(1, NZ):
        p = lax.rem(z + i, NZ)
        put(lent_sum.at[p], lent_z.at[z], pair_send.at[2], pair_recv.at[2], plane(i))
    own_z[z] = own[z]
    await_bytes(own_z.at[pl.ds(0, NZ - 1)], pair_recv.at[1])
    own_sum[...] = jnp.sum(own_z[...], axis=0)
    for i in range(1, NX):
        p = lax.rem(x + i, NX)
        put(own_sum.at[p], own_x.at[x], pair_send.at[3], pair_recv.at[3], plane(i * NZ))
    lent_z[z] = lent_sum[z]
    await_bytes(lent_z.at[pl.ds(0, NZ - 1)], pair_recv.at[2])
    shared[tile, 1] = jnp.sum(lent_z[...], axis=0)
    for i in range(1, NT):
        put(shared.at[tile, 1], shared.at[tile, 1], send.at[4], recv.at[4], other_tile(i))
    own_x[x] = own_sum[x]
    await_bytes(own_x.at[pl.ds(0, NX - 1)], pair_recv.at[3])
    shared[tile, 0] = (own_x[0] + own_x[1]) + (own_x[2] + own_x[3])
    for i in range(1, NT):
        put(shared.at[tile, 0], shared.at[tile, 0], send.at[8], recv.at[8], other_tile(i))
    misfit_tiles[tile] = misfit_row[...]
    await_bytes(misfit_tiles.at[pl.ds(0, NT - 1)], recv.at[7])
    misfit_sum[...] = jnp.sum(misfit_tiles[...], axis=0)
    for i in range(1, NF):
        put(misfit_sum, misfit_rows.at[f], send.at[3], recv.at[3], plane(i))
    await_bytes(partners.at[pl.ds(0, NT - 1)], recv.at[6])
    await_bytes(shared.at[pl.ds(0, NT - 1), 1], recv.at[4])
    await_bytes(shared.at[pl.ds(0, NT - 1), 0], recv.at[8])

    def gradient_of(t, own_rows):
        for lender in range(NT):
            own_rows = own_rows + jnp.where(partners[lender][:, 0:1] == t, shared[lender, 1], 0.0)
        return own_rows

    squares = jnp.zeros_like(models_ref)
    for t in range(NT):
        rows_of = gradient_of(float(t), shared[t, 0])
        squares = squares + rows_of * rows_of
    square_row[...] = jnp.sum(squares, axis=0, keepdims=True)
    for i in range(1, NF):
        put(square_row, square_rows.at[f], send.at[5], recv.at[5], plane(i))
    gradient_ref[...] = gradient_of(tile.astype(F32), shared[tile, 0])
    square_rows[f] = square_row[...]
    misfit_rows[f] = misfit_sum[...]
    await_bytes(misfit_rows.at[pl.ds(0, NF - 1)], recv.at[3])
    members = misfit_row.shape[1]
    final_ref[:, pl.ds(members, members)] = jnp.sum(misfit_rows[...], axis=0)
    await_bytes(square_rows.at[pl.ds(0, NF - 1)], recv.at[5])
    final_ref[:, pl.ds(0, members)] = jnp.sum(square_rows[...], axis=0)

    for c in range(chunks):
        await_bytes(buf.at[c, pl.ds(0, NF - 1)], bulk_send.at[c])
    await_bytes(tiles.at[pl.ds(0, NT - 1)], send.at[0])
    for step in range(1, NZ // 2 + 1):
        passed(step, ring_send)
    await_bytes(gathered.at[pl.ds(0, NX - 1)], send.at[2])
    await_bytes(misfit_rows.at[pl.ds(0, NF - 1)], send.at[3])
    await_bytes(shared.at[pl.ds(0, NT - 1), 1], send.at[4])
    await_bytes(shared.at[pl.ds(0, NT - 1), 0], send.at[8])
    await_bytes(misfit_tiles.at[pl.ds(0, NT - 1)], send.at[7])
    await_bytes(square_rows.at[pl.ds(0, NF - 1)], send.at[5])
    await_bytes(partners.at[pl.ds(0, NT - 1)], send.at[6])
    await_bytes(lent_x.at[pl.ds(0, NX - 1)], pair_send.at[0])
    await_bytes(own_z.at[pl.ds(0, NZ - 1)], pair_send.at[1])
    await_bytes(lent_z.at[pl.ds(0, NZ - 1)], pair_send.at[2])
    await_bytes(own_x.at[pl.ds(0, NX - 1)], pair_send.at[3])


def finish(total, ncells, models_ref, gradient_ref, final_ref, out_ref, misfit_ref):
    members = models_ref.shape[1]
    misfit = final_ref[:, pl.ds(members, members)] / (2.0 * total)
    scale = jnp.sqrt(final_ref[:, pl.ds(0, members)] / ncells + EPSILON)
    out_ref[...] = models_ref[...] - STEP_LENGTH * (misfit / scale) * gradient_ref[...]
    misfit_ref[...] = misfit


def body(sensitivity, models, observed, waveform, cell_index, gate_index):
    owned, members = models.shape
    gates = gate_index.shape[0]
    ncell = cell_index.shape[1]
    chunks = sensitivity.shape[3] // NF // ROWS
    table = jnp.asarray(kernel_table(NF, waveform.shape[0]))
    hbm, vmem = pl.BlockSpec(memory_space=pl.ANY), pl.BlockSpec(memory_space=pltpu.VMEM)
    dma = pltpu.SemaphoreType.DMA
    gradient, final = pl.pallas_call(
        kernel,
        out_shape=(jax.ShapeDtypeStruct((owned, members), F32), jax.ShapeDtypeStruct((1, 2 * members), F32)),
        in_specs=[hbm] * 7,
        out_specs=(vmem, vmem),
        scratch_shapes=[
            pltpu.SMEM(waveform.shape, F32),
            pltpu.SMEM(gate_index.shape, jnp.int32),
            pltpu.VMEM(models.shape, F32),
            pltpu.VMEM((observed.shape[2], gates), F32),
            pltpu.VMEM(cell_index.shape, jnp.int32),
            pltpu.VMEM(table.shape, F32),
            pltpu.VMEM((chunks, NF, 2, ROWS, ncell), F32),
            pltpu.VMEM((NT, ROWS, members), F32),
            pltpu.VMEM((NX, NZ, 2, ROWS, members), F32),
            pltpu.VMEM((2, gates * ROWS, 2 * NF * ROWS), BF16),
            pltpu.VMEM((gates * ROWS, chunks * ROWS), F32),
            pltpu.VMEM((ncell, ncell), BF16),
            pltpu.VMEM((2, members, ncell), BF16),
            pltpu.VMEM((members, gates * ROWS), F32),
            pltpu.VMEM((members, ncell), F32),
            pltpu.VMEM((NX, NZ, ROWS, members), F32),
            pltpu.VMEM((NX, NZ, ROWS, members), F32),
            pltpu.VMEM((NZ, ROWS, members), F32),
            pltpu.VMEM((NZ, ROWS, members), F32),
            pltpu.VMEM((NZ, NX, ROWS, members), F32),
            pltpu.VMEM((NZ, NX, ROWS, members), F32),
            pltpu.VMEM((NX, ROWS, members), F32),
            pltpu.VMEM((NX, ROWS, members), F32),
            pltpu.VMEM((NT, 2, ROWS, members), F32),
            pltpu.VMEM((1, 128), F32),
            pltpu.VMEM((NT, 1, 128), F32),
            pltpu.VMEM((1, members), F32),
            pltpu.VMEM((NF, 1, members), F32),
            pltpu.VMEM((1, members), F32),
            pltpu.VMEM((NT, 1, members), F32),
            pltpu.VMEM((1, members), F32),
            pltpu.VMEM((NF, 1, members), F32),
            dma((chunks,)), dma((chunks,)), dma((9,)), dma((9,)), dma((4,)), dma((4,)), dma((6,)), pltpu.SemaphoreType.REGULAR((2,)), dma((NZ // 2,)), dma((NZ // 2,)),
        ],
        compiler_params=pltpu.CompilerParams(collective_id=0, has_side_effects=True, vmem_limit_bytes=60 << 20),
    )(waveform, gate_index, sensitivity, models, jnp.swapaxes(observed, 1, 2), cell_index, table)
    devices = NT * NF
    updated, misfit = pl.pallas_call(
        functools.partial(finish, NT * sensitivity.shape[3] * gates, owned * devices),
        out_shape=(jax.ShapeDtypeStruct((owned, members), F32), jax.ShapeDtypeStruct((1, members), F32)),
        in_specs=[vmem] * 3,
        out_specs=(vmem, vmem),
    )(models, gradient, final)
    return updated, misfit[0]


def solution(mesh):
    in_specs = (
        P("tile", "freq", None, None, None),
        P(("tile", "freq"), None),
        P("tile", None, "freq"),
        P(),
        P("tile", None),
        P(),
    )
    out_specs = (P(("tile", "freq"), None), P())
    return jax.shard_map(body, mesh=mesh, in_specs=in_specs, out_specs=out_specs, check_vma=False)
```

```python
import functools
import math

import jax
import jax.numpy as jnp
import numpy as np
from jax import lax
from jax.experimental import pallas as pl
from jax.experimental.pallas import tpu as pltpu
from jax.sharding import PartitionSpec as P

HIGH = lax.Precision.HIGHEST
PHASE_RATE = 0.37
STEP_LENGTH = 0.5
EPSILON = 1e-06
MESH = pl.DeviceIdType.MESH
NX, NZ, NT = 4, 8, 8
NF = NX * NZ
ROWS = 8
F32, BF16 = jnp.float32, jnp.bfloat16
STAGES = ((0, 2, 0, 2), (2, 1, 4, 5))
NEAR_Z, FAR_Z, ALONG_X = [1, 2, NZ - 2, NZ - 1], [3, 4, 5], [NZ, 2 * NZ, 3 * NZ]


def kernel_table(freqs, samples):
    freq_col = np.arange(freqs, dtype=np.float32)[:, None] + np.float32(0.5)
    time_row = np.arange(samples, dtype=np.float32)[None, :] + np.float32(0.5)
    phases = ((np.float32(PHASE_RATE) * freq_col) * time_row).astype(np.float64)
    table = np.stack([np.cos(phases), np.sin(phases)], axis=1) / math.sqrt(freqs)
    return table.reshape(2 * freqs, samples).astype(np.float32)


def nn(a, b, precision=None):
    return lax.dot_general(a, b, (((1,), (0,)), ((), ())), precision=precision, preferred_element_type=F32)


def nt(a, b, precision=None):
    return lax.dot_general(a, b, (((1,), (1,)), ((), ())), precision=precision, preferred_element_type=F32)


def split(a):
    high = a.astype(BF16)
    return high, (a - high.astype(F32)).astype(BF16)


def three(dot, a, b):
    return dot(a[0], b[0]) + dot(a[0], b[1]) + dot(a[1], b[0])


def iota(shape, dim):
    return lax.broadcasted_iota(jnp.int32, shape, dim)


def await_bytes(ref, sem):
    pltpu.make_async_copy(ref, ref, sem).wait()


def kernel(
    wave_in, gate_in, sens_ref, models_in, obs_in, cell_in, table_in,
    gradient_ref, final_ref,
    wave_ref, gate_ref, models_ref, obs_ref, cell_ref, table_ref,
    buf, tiles, gathered, wide, expanded, onehot, model_t, rows_ref, cells_t, major, major_x, major_sum, major_z,
    minor, minor_z, minor_sum, minor_x,
    shared, partner_row, partners,
    square_row, square_rows, misfit_row, misfit_tiles, misfit_sum, misfit_rows,
    bulk_send, bulk_recv, send, recv, pair_send, pair_recv, load, known, ring_send, ring_recv,
):
    tile = lax.axis_index("tile")
    f = lax.axis_index("freq")
    x, z = f // NZ, lax.rem(f, NZ)
    chunks = buf.shape[0]
    soundings = chunks * ROWS
    gates = obs_ref.shape[1]

    def plane(i):
        return {"freq": lax.rem(x + i // NZ, NX) * NZ + lax.rem(z + i % NZ, NZ)}

    def other_tile(i):
        return {"tile": lax.rem(tile + i, NT)}

    def put(src, dst, send_sem, recv_sem, device):
        pltpu.make_async_remote_copy(
            src_ref=src, dst_ref=dst, send_sem=send_sem, recv_sem=recv_sem, device_id=device, device_id_type=MESH
        ).start()

    loads = [
        pltpu.make_async_copy(src, dst, load.at[i])
        for i, (src, dst) in enumerate((
            (models_in, models_ref), (cell_in, cell_ref), (gate_in, gate_ref),
            (wave_in, wave_ref), (table_in, table_ref), (obs_in.at[0], obs_ref),
        ))
    ]
    for copy in loads:
        copy.start()
    barrier = pltpu.get_barrier_semaphore()
    for i in NEAR_Z + ALONG_X:
        pl.semaphore_signal(barrier, inc=1, device_id=plane(i), device_id_type=MESH)
    for i in range(1, NT):
        pl.semaphore_signal(barrier, inc=1, device_id=other_tile(i), device_id_type=MESH)
    loads[0].wait()
    pl.semaphore_wait(barrier, len(NEAR_Z + ALONG_X) + NT - 1)

    for i in range(1, NT):
        put(models_ref, tiles.at[tile], send.at[0], recv.at[0], other_tile(i))

    def send_chunk(c, peers=range(1, NF)):
        for i in peers:
            p = plane(i)
            start = pl.multiple_of(p["freq"] * soundings + c * ROWS, ROWS)
            put(sens_ref.at[0, 0, :, pl.ds(start, ROWS), :], buf.at[c, f], bulk_send.at[c], bulk_recv.at[c], p)

    def keep_chunk(c):
        start = pl.multiple_of(f * soundings + c * ROWS, ROWS)
        pltpu.make_async_copy(sens_ref.at[0, 0, :, pl.ds(start, ROWS), :], buf.at[c, f], bulk_recv.at[c]).start()

    send_chunk(0, NEAR_Z + ALONG_X)
    for i in (2, NZ - 2):
        pl.semaphore_signal(known.at[0], inc=1, device_id=plane(i), device_id_type=MESH)
    pl.semaphore_wait(known.at[0], 2)
    for i in ALONG_X:
        pl.semaphore_signal(known.at[1], inc=1, device_id=plane(i), device_id_type=MESH)
    send_chunk(0, FAR_Z)
    pl.semaphore_wait(known.at[1], len(ALONG_X))
    send_chunk(0, [i for i in range(1, NF) if i not in NEAR_Z + ALONG_X + FAR_Z])
    for c in range(chunks):
        keep_chunk(c)

    for copy in loads[1:]:
        copy.wait()
    cells = cell_ref[...]
    block = lax.shift_right_logical(cells, 8)
    partner = jnp.max(jnp.where(block != tile, block, -1), axis=1, keepdims=True)
    local = jnp.where(block == tile, cells & 255, 256 + (cells & 255))
    ncell = cells.shape[1]
    onehot[...] = jnp.where(iota((ncell, ncell), 0) == local, 1.0, 0.0).astype(BF16)

    partner_row[...] = jnp.broadcast_to(partner.astype(F32), partner_row.shape)
    for i in range(1, NT):
        put(partner_row, partners.at[tile], send.at[6], recv.at[6], other_tile(i))
    partners[tile] = partner_row[...]
    tiles[tile] = models_ref[...]
    await_bytes(tiles.at[pl.ds(0, NT - 1)], recv.at[0])
    borrowed = jnp.zeros_like(models_ref)
    for t in range(NT):
        borrowed = jnp.where(partner == t, tiles[t], borrowed)
    gathered[x, z, 0] = models_ref[...]
    gathered[x, z, 1] = borrowed

    def pass_on(step):
        down, up = lax.rem(z - step + 1 + NZ, NZ), lax.rem(z + step - 1, NZ)
        for to, block_z, part in ((1, down, 0), (NZ - 1, up, 1)):
            block_ref = gathered.at[x, block_z] if 2 * step < NZ else gathered.at[x, block_z, part]
            put(block_ref, block_ref, ring_send.at[step - 1], ring_recv.at[step - 1], plane(to))

    def passed(step, sems):
        await_bytes(gathered.at[0, pl.ds(0, 2)] if 2 * step < NZ else gathered.at[0, 0], sems.at[step - 1])

    pass_on(1)
    first, second = range(1, NF // 2), range(NF // 2, NF)
    send_chunk(1, first)

    samples = table_ref.shape[1]
    rows = iota((gates, samples), 0)
    lag = lax.fori_loop(0, gates, lambda g, a: jnp.where(rows == g, gate_ref[g], a), jnp.zeros((gates, samples), jnp.int32))
    lag = lag - iota((gates, samples), 1)
    toeplitz = lax.fori_loop(
        0, samples, lambda k, a: jnp.where(lag == k, wave_ref[k], a), jnp.zeros((gates, samples), F32)
    )
    narrow = nt(toeplitz, table_ref[...], HIGH)
    spread = jnp.where(lax.shift_right_logical(iota((gates * ROWS, gates), 0), 3) == iota((gates * ROWS, gates), 1), 1.0, 0.0)
    fps = narrow.shape[1]
    pick = jnp.where(iota((fps, fps * ROWS), 0) == lax.shift_right_logical(iota((fps, fps * ROWS), 1), 3), 1.0, 0.0)
    big = nn(nn(spread, narrow, HIGH), pick, HIGH)
    same = (iota(big.shape, 0) & 7) == (iota(big.shape, 1) & 7)
    big_high, big_low = split(jnp.where(same, big, 0.0))
    wide[0] = big_high
    wide[1] = big_low
    expanded[...] = nt(spread, obs_ref[...], HIGH)

    passed(1, ring_recv)
    pass_on(2)
    send_chunk(1, second)
    passed(2, ring_recv)
    pass_on(3)
    send_chunk(2, first)
    passed(3, ring_recv)
    pass_on(4)
    send_chunk(2, second)
    passed(4, ring_recv)
    for i in range(1, NX):
        put(gathered.at[x], gathered.at[x], send.at[2], recv.at[2], plane(i * NZ))
    send_chunk(3)

    await_bytes(gathered.at[pl.ds(0, NX - 1)], recv.at[2])
    for b in range(2):
        part = gathered[:, :, b].reshape(NF * ROWS, -1)
        part_high, part_low = split(part.T)
        hot = onehot[pl.ds(b * NF * ROWS, NF * ROWS), :]
        if b == 0:
            model_high, model_low = nn(part_high, hot), nn(part_low, hot)
        else:
            model_high, model_low = model_high + nn(part_high, hot), model_low + nn(part_low, hot)
    model_t[0] = model_high.astype(BF16)
    model_t[1] = model_low.astype(BF16)

    cells_t[...] = jnp.zeros_like(cells_t)
    misfit_row[...] = jnp.zeros_like(misfit_row)

    rows_ref[...] = jnp.zeros_like(rows_ref)

    def add_squares():
        rows_t = rows_ref[...]
        misfit_row[...] += nt(jnp.ones((8, rows_t.shape[1]), F32), rows_t * rows_t, HIGH)[0:1]

    def chunk(c, carry):
        add_squares()
        seen = expanded[...]
        seen = jnp.where(iota(seen.shape, 1) == c * ROWS + (iota(seen.shape, 0) & 7), seen, 0.0)
        seen_row = nt(jnp.ones((8, seen.shape[1]), F32), seen, HIGH)[0:1]
        await_bytes(buf.at[c], bulk_recv.at[c])
        block_s = split(buf[c].reshape(fps * ROWS, ncell))
        operator = split(three(nn, (wide[0], wide[1]), block_s))
        rows_t = three(nt, (model_t[0], model_t[1]), operator) - seen_row
        rows_ref[...] = rows_t
        cells_t[...] += three(nn, split(rows_t), operator)
        return carry

    lax.fori_loop(0, chunks, chunk, 0)

    grad_high, grad_low = split(cells_t[...])
    half, lanes = NF * ROWS, cells_t.shape[0] // 2

    def global_rows(b):
        hot = onehot[pl.ds(b * half, half), :]
        return (nt(hot, grad_high) + nt(hot, grad_low)).reshape(NX, NZ, ROWS, -1)

    lent = global_rows(1)
    major[:, 0] = lent[..., :lanes]
    major[:, 1] = lent[..., lanes:]
    for i in range(1, NX):
        p = lax.rem(x + i, NX)
        put(major.at[p, pl.ds(0, 2)], major_x.at[x, pl.ds(0, 2)], pair_send.at[0], pair_recv.at[0], plane(i * NZ))
    own = global_rows(0)
    minor[...] = jnp.swapaxes(own[..., lanes:], 0, 1)
    for i in range(1, NZ):
        p = lax.rem(z + i, NZ)
        put(minor.at[p], minor_z.at[z], pair_send.at[1], pair_recv.at[1], plane(i))
    major[:, 2] = own[..., :lanes]
    for i in range(1, NX):
        p = lax.rem(x + i, NX)
        put(major.at[p, 2], major_x.at[x, 2], pair_send.at[4], pair_recv.at[4], plane(i * NZ))
    add_squares()
    for i in range(1, NT):
        put(misfit_row, misfit_tiles.at[tile], send.at[7], recv.at[7], other_tile(i))

    major_x[x] = major[x]
    minor_z[z] = minor[z]
    for first, count, sem_x, sem_z in STAGES:
        quarters = pl.ds(first, count)
        await_bytes(major_x.at[pl.ds(0, NX - 1), quarters], pair_recv.at[sem_x])
        total_x = (major_x[0, quarters] + major_x[1, quarters]) + (major_x[2, quarters] + major_x[3, quarters])
        major_sum[:, quarters] = jnp.swapaxes(total_x, 0, 1)
        for i in range(1, NZ):
            p = lax.rem(z + i, NZ)
            put(major_sum.at[p, quarters], major_z.at[z, quarters], pair_send.at[sem_z], pair_recv.at[sem_z], plane(i))
    await_bytes(minor_z.at[pl.ds(0, NZ - 1)], pair_recv.at[1])
    minor_sum[...] = jnp.sum(minor_z[...], axis=0)
    for i in range(1, NX):
        p = lax.rem(x + i, NX)
        put(minor_sum.at[p], minor_x.at[x], pair_send.at[3], pair_recv.at[3], plane(i * NZ))
    minor_x[x] = minor_sum[x]
    await_bytes(minor_x.at[pl.ds(0, NX - 1)], pair_recv.at[3])
    shared[tile, 0, :, pl.ds(lanes, lanes)] = (minor_x[0] + minor_x[1]) + (minor_x[2] + minor_x[3])
    major_z[z] = major_sum[z]
    for first, count, _, sem_z in STAGES:
        await_bytes(major_z.at[pl.ds(0, NZ - 1), pl.ds(first, count)], pair_recv.at[sem_z])
    total_z = jnp.sum(major_z[...], axis=0)
    shared[tile, 1, :, pl.ds(0, lanes)] = total_z[0]
    shared[tile, 1, :, pl.ds(lanes, lanes)] = total_z[1]
    shared[tile, 0, :, pl.ds(0, lanes)] = total_z[2]
    for i in range(1, NT):
        put(shared.at[tile], shared.at[tile], send.at[4], recv.at[4], other_tile(i))
    misfit_tiles[tile] = misfit_row[...]
    await_bytes(misfit_tiles.at[pl.ds(0, NT - 1)], recv.at[7])
    misfit_sum[...] = jnp.sum(misfit_tiles[...], axis=0)
    for i in range(1, NF):
        put(misfit_sum, misfit_rows.at[f], send.at[3], recv.at[3], plane(i))
    await_bytes(partners.at[pl.ds(0, NT - 1)], recv.at[6])
    await_bytes(shared.at[pl.ds(0, NT - 1)], recv.at[4])

    def gradient_of(t, own_rows):
        for lender in range(NT):
            own_rows = own_rows + jnp.where(partners[lender][:, 0:1] == t, shared[lender, 1], 0.0)
        return own_rows

    squares = jnp.zeros_like(models_ref)
    for t in range(NT):
        rows_of = gradient_of(float(t), shared[t, 0])
        squares = squares + rows_of * rows_of
    square_row[...] = jnp.sum(squares, axis=0, keepdims=True)
    for i in range(1, NF):
        put(square_row, square_rows.at[f], send.at[5], recv.at[5], plane(i))
    gradient_ref[...] = gradient_of(tile.astype(F32), shared[tile, 0])
    square_rows[f] = square_row[...]
    misfit_rows[f] = misfit_sum[...]
    await_bytes(misfit_rows.at[pl.ds(0, NF - 1)], recv.at[3])
    members = misfit_row.shape[1]
    final_ref[:, pl.ds(members, members)] = jnp.sum(misfit_rows[...], axis=0)
    await_bytes(square_rows.at[pl.ds(0, NF - 1)], recv.at[5])
    final_ref[:, pl.ds(0, members)] = jnp.sum(square_rows[...], axis=0)

    for c in range(chunks):
        await_bytes(buf.at[c, pl.ds(0, NF - 1)], bulk_send.at[c])
    await_bytes(tiles.at[pl.ds(0, NT - 1)], send.at[0])
    for step in range(1, NZ // 2 + 1):
        passed(step, ring_send)
    await_bytes(gathered.at[pl.ds(0, NX - 1)], send.at[2])
    await_bytes(misfit_rows.at[pl.ds(0, NF - 1)], send.at[3])
    await_bytes(shared.at[pl.ds(0, NT - 1)], send.at[4])
    await_bytes(misfit_tiles.at[pl.ds(0, NT - 1)], send.at[7])
    await_bytes(square_rows.at[pl.ds(0, NF - 1)], send.at[5])
    await_bytes(partners.at[pl.ds(0, NT - 1)], send.at[6])
    for first, count, sem_x, sem_z in STAGES:
        await_bytes(major_x.at[pl.ds(0, NX - 1), pl.ds(first, count)], pair_send.at[sem_x])
        await_bytes(major_z.at[pl.ds(0, NZ - 1), pl.ds(first, count)], pair_send.at[sem_z])
    await_bytes(minor_z.at[pl.ds(0, NZ - 1)], pair_send.at[1])
    await_bytes(minor_x.at[pl.ds(0, NX - 1)], pair_send.at[3])


def finish(total, ncells, models_ref, gradient_ref, final_ref, out_ref, misfit_ref):
    members = models_ref.shape[1]
    misfit = final_ref[:, pl.ds(members, members)] / (2.0 * total)
    scale = jnp.sqrt(final_ref[:, pl.ds(0, members)] / ncells + EPSILON)
    out_ref[...] = models_ref[...] - STEP_LENGTH * (misfit / scale) * gradient_ref[...]
    misfit_ref[...] = misfit


def body(sensitivity, models, observed, waveform, cell_index, gate_index):
    owned, members = models.shape
    gates = gate_index.shape[0]
    ncell = cell_index.shape[1]
    chunks = sensitivity.shape[3] // NF // ROWS
    table = jnp.asarray(kernel_table(NF, waveform.shape[0]))
    hbm, vmem = pl.BlockSpec(memory_space=pl.ANY), pl.BlockSpec(memory_space=pltpu.VMEM)
    dma = pltpu.SemaphoreType.DMA
    gradient, final = pl.pallas_call(
        kernel,
        out_shape=(jax.ShapeDtypeStruct((owned, members), F32), jax.ShapeDtypeStruct((1, 2 * members), F32)),
        in_specs=[hbm] * 7,
        out_specs=(vmem, vmem),
        scratch_shapes=[
            pltpu.SMEM(waveform.shape, F32),
            pltpu.SMEM(gate_index.shape, jnp.int32),
            pltpu.VMEM(models.shape, F32),
            pltpu.VMEM((observed.shape[2], gates), F32),
            pltpu.VMEM(cell_index.shape, jnp.int32),
            pltpu.VMEM(table.shape, F32),
            pltpu.VMEM((chunks, NF, 2, ROWS, ncell), F32),
            pltpu.VMEM((NT, ROWS, members), F32),
            pltpu.VMEM((NX, NZ, 2, ROWS, members), F32),
            pltpu.VMEM((2, gates * ROWS, 2 * NF * ROWS), BF16),
            pltpu.VMEM((gates * ROWS, chunks * ROWS), F32),
            pltpu.VMEM((ncell, ncell), BF16),
            pltpu.VMEM((2, members, ncell), BF16),
            pltpu.VMEM((members, gates * ROWS), F32),
            pltpu.VMEM((members, ncell), F32),
            pltpu.VMEM((NX, 3, NZ, ROWS, members // 2), F32),
            pltpu.VMEM((NX, 3, NZ, ROWS, members // 2), F32),
            pltpu.VMEM((NZ, 3, ROWS, members // 2), F32),
            pltpu.VMEM((NZ, 3, ROWS, members // 2), F32),
            pltpu.VMEM((NZ, NX, ROWS, members // 2), F32),
            pltpu.VMEM((NZ, NX, ROWS, members // 2), F32),
            pltpu.VMEM((NX, ROWS, members // 2), F32),
            pltpu.VMEM((NX, ROWS, members // 2), F32),
            pltpu.VMEM((NT, 2, ROWS, members), F32),
            pltpu.VMEM((1, 128), F32),
            pltpu.VMEM((NT, 1, 128), F32),
            pltpu.VMEM((1, members), F32),
            pltpu.VMEM((NF, 1, members), F32),
            pltpu.VMEM((1, members), F32),
            pltpu.VMEM((NT, 1, members), F32),
            pltpu.VMEM((1, members), F32),
            pltpu.VMEM((NF, 1, members), F32),
            dma((chunks,)), dma((chunks,)), dma((8,)), dma((8,)), dma((6,)), dma((6,)), dma((6,)), pltpu.SemaphoreType.REGULAR((2,)), dma((NZ // 2,)), dma((NZ // 2,)),
        ],
        compiler_params=pltpu.CompilerParams(collective_id=0, has_side_effects=True, vmem_limit_bytes=60 << 20),
    )(waveform, gate_index, sensitivity, models, jnp.swapaxes(observed, 1, 2), cell_index, table)
    devices = NT * NF
    updated, misfit = pl.pallas_call(
        functools.partial(finish, NT * sensitivity.shape[3] * gates, owned * devices),
        out_shape=(jax.ShapeDtypeStruct((owned, members), F32), jax.ShapeDtypeStruct((1, members), F32)),
        in_specs=[vmem] * 3,
        out_specs=(vmem, vmem),
    )(models, gradient, final)
    return updated, misfit[0]


def solution(mesh):
    in_specs = (
        P("tile", "freq", None, None, None),
        P(("tile", "freq"), None),
        P("tile", None, "freq"),
        P(),
        P("tile", None),
        P(),
    )
    out_specs = (P(("tile", "freq"), None), P())
    return jax.shard_map(body, mesh=mesh, in_specs=in_specs, out_specs=out_specs, check_vma=False)
```

```python
import functools
import math

import jax
import jax.numpy as jnp
import numpy as np
from jax import lax
from jax.experimental import pallas as pl
from jax.experimental.pallas import tpu as pltpu
from jax.sharding import PartitionSpec as P

HIGH = lax.Precision.HIGHEST
PHASE_RATE = 0.37
STEP_LENGTH = 0.5
EPSILON = 1e-06
MESH = pl.DeviceIdType.MESH
NX, NZ, NT = 4, 8, 8
NF = NX * NZ
ROWS = 8
F32, BF16 = jnp.float32, jnp.bfloat16
EARLY = range(NZ, 3 * NZ)
FAR_FIRST = sorted(range(1, NF), key=lambda i: (-min(i % NZ, NZ - i % NZ), -min(i // NZ, NX - i // NZ), i))
STAGES = ((0, 2, 0, 2), (2, 1, 4, 5))
NEAR_Z, FAR_Z, ALONG_X = [1, 2, NZ - 2, NZ - 1], [3, 4, 5], [NZ, 2 * NZ, 3 * NZ]


def kernel_table(freqs, samples):
    freq_col = np.arange(freqs, dtype=np.float32)[:, None] + np.float32(0.5)
    time_row = np.arange(samples, dtype=np.float32)[None, :] + np.float32(0.5)
    phases = ((np.float32(PHASE_RATE) * freq_col) * time_row).astype(np.float64)
    table = np.stack([np.cos(phases), np.sin(phases)], axis=1) / math.sqrt(freqs)
    return table.reshape(2 * freqs, samples).astype(np.float32)


def nn(a, b, precision=None):
    return lax.dot_general(a, b, (((1,), (0,)), ((), ())), precision=precision, preferred_element_type=F32)


def nt(a, b, precision=None):
    return lax.dot_general(a, b, (((1,), (1,)), ((), ())), precision=precision, preferred_element_type=F32)


def split(a):
    high = a.astype(BF16)
    return high, (a - high.astype(F32)).astype(BF16)


def three(dot, a, b):
    return dot(a[0], b[0]) + dot(a[0], b[1]) + dot(a[1], b[0])


def iota(shape, dim):
    return lax.broadcasted_iota(jnp.int32, shape, dim)


def await_bytes(ref, sem):
    pltpu.make_async_copy(ref, ref, sem).wait()


def kernel(
    wave_in, gate_in, sens_ref, models_in, obs_in, cell_in, table_in,
    gradient_ref, final_ref,
    wave_ref, gate_ref, models_ref, obs_ref, cell_ref, table_ref,
    buf, tiles, gathered, wide, expanded, onehot, model_t, rows_ref, cells_t, major, major_x, major_sum, major_z,
    minor, minor_z, minor_sum, minor_x,
    shared, partner_row, partners,
    square_row, square_rows, misfit_row, misfit_tiles, misfit_sum, misfit_rows,
    bulk_send, bulk_recv, send, recv, pair_send, pair_recv, load, known, ring_send, ring_recv,
):
    tile = lax.axis_index("tile")
    f = lax.axis_index("freq")
    x, z = f // NZ, lax.rem(f, NZ)
    chunks = buf.shape[0]
    soundings = chunks * ROWS
    gates = obs_ref.shape[1]

    def plane(i):
        return {"freq": lax.rem(x + i // NZ, NX) * NZ + lax.rem(z + i % NZ, NZ)}

    def other_tile(i):
        return {"tile": lax.rem(tile + i, NT)}

    def put(src, dst, send_sem, recv_sem, device):
        pltpu.make_async_remote_copy(
            src_ref=src, dst_ref=dst, send_sem=send_sem, recv_sem=recv_sem, device_id=device, device_id_type=MESH
        ).start()

    loads = [
        pltpu.make_async_copy(src, dst, load.at[i])
        for i, (src, dst) in enumerate((
            (models_in, models_ref), (cell_in, cell_ref), (gate_in, gate_ref),
            (wave_in, wave_ref), (table_in, table_ref), (obs_in.at[0], obs_ref),
        ))
    ]
    for copy in loads:
        copy.start()
    barrier = pltpu.get_barrier_semaphore()
    for i in NEAR_Z + ALONG_X:
        pl.semaphore_signal(barrier, inc=1, device_id=plane(i), device_id_type=MESH)
    for i in range(1, NT):
        pl.semaphore_signal(barrier, inc=1, device_id=other_tile(i), device_id_type=MESH)
    loads[0].wait()
    pl.semaphore_wait(barrier, len(NEAR_Z + ALONG_X) + NT - 1)

    for i in range(1, NT):
        put(models_ref, tiles.at[tile], send.at[0], recv.at[0], other_tile(i))

    def send_chunk(c, peers=range(1, NF)):
        for i in peers:
            p = plane(i)
            start = pl.multiple_of(p["freq"] * soundings + c * ROWS, ROWS)
            put(sens_ref.at[0, 0, :, pl.ds(start, ROWS), :], buf.at[c, f], bulk_send.at[c], bulk_recv.at[c, int(i not in EARLY)], p)

    def keep_chunk(c):
        start = pl.multiple_of(f * soundings + c * ROWS, ROWS)
        pltpu.make_async_copy(sens_ref.at[0, 0, :, pl.ds(start, ROWS), :], buf.at[c, f], bulk_recv.at[c, 1]).start()

    send_chunk(0, NEAR_Z + ALONG_X)
    for i in (2, NZ - 2):
        pl.semaphore_signal(known.at[0], inc=1, device_id=plane(i), device_id_type=MESH)
    pl.semaphore_wait(known.at[0], 2)
    for i in ALONG_X:
        pl.semaphore_signal(known.at[1], inc=1, device_id=plane(i), device_id_type=MESH)
    send_chunk(0, FAR_Z)
    pl.semaphore_wait(known.at[1], len(ALONG_X))
    send_chunk(0, [i for i in range(1, NF) if i not in NEAR_Z + ALONG_X + FAR_Z])
    for c in range(chunks):
        keep_chunk(c)

    for copy in loads[1:]:
        copy.wait()
    cells = cell_ref[...]
    block = lax.shift_right_logical(cells, 8)
    partner = jnp.max(jnp.where(block != tile, block, -1), axis=1, keepdims=True)
    local = jnp.where(block == tile, cells & 255, 256 + (cells & 255))
    ncell = cells.shape[1]
    onehot[...] = jnp.where(iota((ncell, ncell), 0) == local, 1.0, 0.0).astype(BF16)

    partner_row[...] = jnp.broadcast_to(partner.astype(F32), partner_row.shape)
    for i in range(1, NT):
        put(partner_row, partners.at[tile], send.at[6], recv.at[6], other_tile(i))
    partners[tile] = partner_row[...]
    tiles[tile] = models_ref[...]
    await_bytes(tiles.at[pl.ds(0, NT - 1)], recv.at[0])
    borrowed = jnp.zeros_like(models_ref)
    for t in range(NT):
        borrowed = jnp.where(partner == t, tiles[t], borrowed)
    gathered[x, z, 0] = models_ref[...]
    gathered[x, z, 1] = borrowed

    def pass_on(step):
        down, up = lax.rem(z - step + 1 + NZ, NZ), lax.rem(z + step - 1, NZ)
        for to, block_z, part in ((1, down, 0), (NZ - 1, up, 1)):
            block_ref = gathered.at[x, block_z] if 2 * step < NZ else gathered.at[x, block_z, part]
            put(block_ref, block_ref, ring_send.at[step - 1], ring_recv.at[step - 1], plane(to))

    def passed(step, sems):
        await_bytes(gathered.at[0, pl.ds(0, 2)] if 2 * step < NZ else gathered.at[0, 0], sems.at[step - 1])

    pass_on(1)
    first, second = range(1, NF // 2), range(NF // 2, NF)
    send_chunk(1, first)

    samples = table_ref.shape[1]
    rows = iota((gates, samples), 0)
    lag = lax.fori_loop(0, gates, lambda g, a: jnp.where(rows == g, gate_ref[g], a), jnp.zeros((gates, samples), jnp.int32))
    lag = lag - iota((gates, samples), 1)
    toeplitz = lax.fori_loop(
        0, samples, lambda k, a: jnp.where(lag == k, wave_ref[k], a), jnp.zeros((gates, samples), F32)
    )
    narrow = nt(toeplitz, table_ref[...], HIGH)
    spread = jnp.where(lax.shift_right_logical(iota((gates * ROWS, gates), 0), 3) == iota((gates * ROWS, gates), 1), 1.0, 0.0)
    fps = narrow.shape[1]
    pick = jnp.where(iota((fps, fps * ROWS), 0) == lax.shift_right_logical(iota((fps, fps * ROWS), 1), 3), 1.0, 0.0)
    big = nn(nn(spread, narrow, HIGH), pick, HIGH)
    same = (iota(big.shape, 0) & 7) == (iota(big.shape, 1) & 7)
    big_high, big_low = split(jnp.where(same, big, 0.0))
    wide[0] = big_high
    wide[1] = big_low
    expanded[...] = nt(spread, obs_ref[...], HIGH)

    passed(1, ring_recv)
    pass_on(2)
    send_chunk(1, second)
    passed(2, ring_recv)
    pass_on(3)
    send_chunk(2, first)
    passed(3, ring_recv)
    pass_on(4)
    send_chunk(2, second)
    passed(4, ring_recv)
    for i in range(1, NX):
        put(gathered.at[x], gathered.at[x], send.at[2], recv.at[2], plane(i * NZ))
    send_chunk(3, sorted(FAR_FIRST, key=lambda i: i not in EARLY))

    await_bytes(gathered.at[pl.ds(0, NX - 1)], recv.at[2])
    for b in range(2):
        part = gathered[:, :, b].reshape(NF * ROWS, -1)
        part_high, part_low = split(part.T)
        hot = onehot[pl.ds(b * NF * ROWS, NF * ROWS), :]
        if b == 0:
            model_high, model_low = nn(part_high, hot), nn(part_low, hot)
        else:
            model_high, model_low = model_high + nn(part_high, hot), model_low + nn(part_low, hot)
    model_t[0] = model_high.astype(BF16)
    model_t[1] = model_low.astype(BF16)

    cells_t[...] = jnp.zeros_like(cells_t)
    misfit_row[...] = jnp.zeros_like(misfit_row)

    rows_ref[...] = jnp.zeros_like(rows_ref)

    def add_squares():
        rows_t = rows_ref[...]
        misfit_row[...] += nt(jnp.ones((8, rows_t.shape[1]), F32), rows_t * rows_t, HIGH)[0:1]

    def chunk(c, carry):
        add_squares()
        seen = expanded[...]
        seen = jnp.where(iota(seen.shape, 1) == c * ROWS + (iota(seen.shape, 0) & 7), seen, 0.0)
        seen_row = nt(jnp.ones((8, seen.shape[1]), F32), seen, HIGH)[0:1]
        operator = None
        for late, offsets in enumerate(((1, 2), (3, 0))):
            await_bytes(buf.at[c, pl.ds(0, NF // 2)], bulk_recv.at[c, late])
            blocks, columns = [], [[], []]
            for offset in offsets:
                source = lax.rem(x - offset + NX, NX)
                width = NZ * 2 * ROWS
                blocks.append(buf[c, pl.ds(source * NZ, NZ)].reshape(width, ncell))
                for k in range(2):
                    columns[k].append(wide[k, :, pl.ds(pl.multiple_of(source * width, width), width)])
            block_s = split(jnp.concatenate(blocks, axis=0))
            part = three(nn, [jnp.concatenate(cols, axis=1) for cols in columns], block_s)
            operator = part if operator is None else operator + part
        operator = split(operator)
        rows_t = three(nt, (model_t[0], model_t[1]), operator) - seen_row
        rows_ref[...] = rows_t
        cells_t[...] += three(nn, split(rows_t), operator)
        return carry

    lax.fori_loop(0, chunks, chunk, 0)

    grad_high, grad_low = split(cells_t[...])
    half, lanes = NF * ROWS, cells_t.shape[0] // 2

    def global_rows(b):
        hot = onehot[pl.ds(b * half, half), :]
        return (nt(hot, grad_high) + nt(hot, grad_low)).reshape(NX, NZ, ROWS, -1)

    lent = global_rows(1)
    major[:, 0] = lent[..., :lanes]
    major[:, 1] = lent[..., lanes:]
    for i in (2, 1, 3):
        p = lax.rem(x + i, NX)
        put(major.at[p, pl.ds(0, 2)], major_x.at[x, pl.ds(0, 2)], pair_send.at[0], pair_recv.at[0], plane(i * NZ))
    own = global_rows(0)
    minor[...] = jnp.swapaxes(own[..., lanes:], 0, 1)
    for i in (4, 3, 5, 2, 6, 1, 7):
        p = lax.rem(z + i, NZ)
        put(minor.at[p], minor_z.at[z], pair_send.at[1], pair_recv.at[1], plane(i))
    major[:, 2] = own[..., :lanes]
    for i in (2, 1, 3):
        p = lax.rem(x + i, NX)
        put(major.at[p, 2], major_x.at[x, 2], pair_send.at[4], pair_recv.at[4], plane(i * NZ))
    add_squares()
    for i in range(1, NT):
        put(misfit_row, misfit_tiles.at[tile], send.at[7], recv.at[7], other_tile(i))

    major_x[x] = major[x]
    minor_z[z] = minor[z]
    for first, count, sem_x, sem_z in STAGES:
        quarters = pl.ds(first, count)
        await_bytes(major_x.at[pl.ds(0, NX - 1), quarters], pair_recv.at[sem_x])
        total_x = (major_x[0, quarters] + major_x[1, quarters]) + (major_x[2, quarters] + major_x[3, quarters])
        major_sum[:, quarters] = jnp.swapaxes(total_x, 0, 1)
        for i in (4, 3, 5, 2, 6, 1, 7):
            p = lax.rem(z + i, NZ)
            put(major_sum.at[p, quarters], major_z.at[z, quarters], pair_send.at[sem_z], pair_recv.at[sem_z], plane(i))
    await_bytes(minor_z.at[pl.ds(0, NZ - 1)], pair_recv.at[1])
    minor_sum[...] = jnp.sum(minor_z[...], axis=0)
    for i in (2, 1, 3):
        p = lax.rem(x + i, NX)
        put(minor_sum.at[p], minor_x.at[x], pair_send.at[3], pair_recv.at[3], plane(i * NZ))
    minor_x[x] = minor_sum[x]
    major_z[z] = major_sum[z]
    await_bytes(major_z.at[pl.ds(0, NZ - 1), pl.ds(0, 2)], pair_recv.at[STAGES[0][3]])
    lent_z = jnp.sum(major_z[:, pl.ds(0, 2)], axis=0)
    shared[tile, 1, :, pl.ds(0, lanes)] = lent_z[0]
    shared[tile, 1, :, pl.ds(lanes, lanes)] = lent_z[1]
    for i in range(1, NT):
        put(shared.at[tile, 1], shared.at[tile, 1], send.at[8], recv.at[8], other_tile(i))
    await_bytes(minor_x.at[pl.ds(0, NX - 1)], pair_recv.at[3])
    shared[tile, 0, :, pl.ds(lanes, lanes)] = (minor_x[0] + minor_x[1]) + (minor_x[2] + minor_x[3])
    await_bytes(major_z.at[pl.ds(0, NZ - 1), pl.ds(2, 1)], pair_recv.at[STAGES[1][3]])
    shared[tile, 0, :, pl.ds(0, lanes)] = jnp.sum(major_z[:, 2], axis=0)
    for i in range(1, NT):
        put(shared.at[tile, 0], shared.at[tile, 0], send.at[4], recv.at[4], other_tile(i))
    misfit_tiles[tile] = misfit_row[...]
    await_bytes(misfit_tiles.at[pl.ds(0, NT - 1)], recv.at[7])
    misfit_sum[...] = jnp.sum(misfit_tiles[...], axis=0)
    for i in range(1, NF):
        put(misfit_sum, misfit_rows.at[f], send.at[3], recv.at[3], plane(i))
    await_bytes(partners.at[pl.ds(0, NT - 1)], recv.at[6])
    await_bytes(shared.at[pl.ds(0, NT - 1), 1], recv.at[8])
    await_bytes(shared.at[pl.ds(0, NT - 1), 0], recv.at[4])

    def gradient_of(t, own_rows):
        for lender in range(NT):
            own_rows = own_rows + jnp.where(partners[lender][:, 0:1] == t, shared[lender, 1], 0.0)
        return own_rows

    squares = jnp.zeros_like(models_ref)
    for t in range(NT):
        rows_of = gradient_of(float(t), shared[t, 0])
        squares = squares + rows_of * rows_of
    square_row[...] = jnp.sum(squares, axis=0, keepdims=True)
    for i in FAR_FIRST:
        put(square_row, square_rows.at[f], send.at[5], recv.at[5], plane(i))
    gradient_ref[...] = gradient_of(tile.astype(F32), shared[tile, 0])
    square_rows[f] = square_row[...]
    misfit_rows[f] = misfit_sum[...]
    await_bytes(misfit_rows.at[pl.ds(0, NF - 1)], recv.at[3])
    members = misfit_row.shape[1]
    final_ref[:, pl.ds(members, members)] = jnp.sum(misfit_rows[...], axis=0)
    await_bytes(square_rows.at[pl.ds(0, NF - 1)], recv.at[5])
    final_ref[:, pl.ds(0, members)] = jnp.sum(square_rows[...], axis=0)

    for c in range(chunks):
        await_bytes(buf.at[c, pl.ds(0, NF - 1)], bulk_send.at[c])
    await_bytes(tiles.at[pl.ds(0, NT - 1)], send.at[0])
    for step in range(1, NZ // 2 + 1):
        passed(step, ring_send)
    await_bytes(gathered.at[pl.ds(0, NX - 1)], send.at[2])
    await_bytes(misfit_rows.at[pl.ds(0, NF - 1)], send.at[3])
    await_bytes(shared.at[pl.ds(0, NT - 1), 1], send.at[8])
    await_bytes(shared.at[pl.ds(0, NT - 1), 0], send.at[4])
    await_bytes(misfit_tiles.at[pl.ds(0, NT - 1)], send.at[7])
    await_bytes(square_rows.at[pl.ds(0, NF - 1)], send.at[5])
    await_bytes(partners.at[pl.ds(0, NT - 1)], send.at[6])
    for first, count, sem_x, sem_z in STAGES:
        await_bytes(major_x.at[pl.ds(0, NX - 1), pl.ds(first, count)], pair_send.at[sem_x])
        await_bytes(major_z.at[pl.ds(0, NZ - 1), pl.ds(first, count)], pair_send.at[sem_z])
    await_bytes(minor_z.at[pl.ds(0, NZ - 1)], pair_send.at[1])
    await_bytes(minor_x.at[pl.ds(0, NX - 1)], pair_send.at[3])


def finish(total, ncells, models_ref, gradient_ref, final_ref, out_ref, misfit_ref):
    members = models_ref.shape[1]
    misfit = final_ref[:, pl.ds(members, members)] / (2.0 * total)
    scale = jnp.sqrt(final_ref[:, pl.ds(0, members)] / ncells + EPSILON)
    out_ref[...] = models_ref[...] - STEP_LENGTH * (misfit / scale) * gradient_ref[...]
    misfit_ref[...] = misfit


def body(sensitivity, models, observed, waveform, cell_index, gate_index):
    owned, members = models.shape
    gates = gate_index.shape[0]
    ncell = cell_index.shape[1]
    chunks = sensitivity.shape[3] // NF // ROWS
    table = jnp.asarray(kernel_table(NF, waveform.shape[0]))
    hbm, vmem = pl.BlockSpec(memory_space=pl.ANY), pl.BlockSpec(memory_space=pltpu.VMEM)
    dma = pltpu.SemaphoreType.DMA
    gradient, final = pl.pallas_call(
        kernel,
        out_shape=(jax.ShapeDtypeStruct((owned, members), F32), jax.ShapeDtypeStruct((1, 2 * members), F32)),
        in_specs=[hbm] * 7,
        out_specs=(vmem, vmem),
        scratch_shapes=[
            pltpu.SMEM(waveform.shape, F32),
            pltpu.SMEM(gate_index.shape, jnp.int32),
            pltpu.VMEM(models.shape, F32),
            pltpu.VMEM((observed.shape[2], gates), F32),
            pltpu.VMEM(cell_index.shape, jnp.int32),
            pltpu.VMEM(table.shape, F32),
            pltpu.VMEM((chunks, NF, 2, ROWS, ncell), F32),
            pltpu.VMEM((NT, ROWS, members), F32),
            pltpu.VMEM((NX, NZ, 2, ROWS, members), F32),
            pltpu.VMEM((2, gates * ROWS, 2 * NF * ROWS), BF16),
            pltpu.VMEM((gates * ROWS, chunks * ROWS), F32),
            pltpu.VMEM((ncell, ncell), BF16),
            pltpu.VMEM((2, members, ncell), BF16),
            pltpu.VMEM((members, gates * ROWS), F32),
            pltpu.VMEM((members, ncell), F32),
            pltpu.VMEM((NX, 3, NZ, ROWS, members // 2), F32),
            pltpu.VMEM((NX, 3, NZ, ROWS, members // 2), F32),
            pltpu.VMEM((NZ, 3, ROWS, members // 2), F32),
            pltpu.VMEM((NZ, 3, ROWS, members // 2), F32),
            pltpu.VMEM((NZ, NX, ROWS, members // 2), F32),
            pltpu.VMEM((NZ, NX, ROWS, members // 2), F32),
            pltpu.VMEM((NX, ROWS, members // 2), F32),
            pltpu.VMEM((NX, ROWS, members // 2), F32),
            pltpu.VMEM((NT, 2, ROWS, members), F32),
            pltpu.VMEM((1, 128), F32),
            pltpu.VMEM((NT, 1, 128), F32),
            pltpu.VMEM((1, members), F32),
            pltpu.VMEM((NF, 1, members), F32),
            pltpu.VMEM((1, members), F32),
            pltpu.VMEM((NT, 1, members), F32),
            pltpu.VMEM((1, members), F32),
            pltpu.VMEM((NF, 1, members), F32),
            dma((chunks,)), dma((chunks, 2)), dma((9,)), dma((9,)), dma((6,)), dma((6,)), dma((6,)), pltpu.SemaphoreType.REGULAR((2,)), dma((NZ // 2,)), dma((NZ // 2,)),
        ],
        compiler_params=pltpu.CompilerParams(collective_id=0, has_side_effects=True, vmem_limit_bytes=60 << 20),
    )(waveform, gate_index, sensitivity, models, jnp.swapaxes(observed, 1, 2), cell_index, table)
    devices = NT * NF
    updated, misfit = pl.pallas_call(
        functools.partial(finish, NT * sensitivity.shape[3] * gates, owned * devices),
        out_shape=(jax.ShapeDtypeStruct((owned, members), F32), jax.ShapeDtypeStruct((1, members), F32)),
        in_specs=[vmem] * 3,
        out_specs=(vmem, vmem),
    )(models, gradient, final)
    return updated, misfit[0]


def solution(mesh):
    in_specs = (
        P("tile", "freq", None, None, None),
        P(("tile", "freq"), None),
        P("tile", None, "freq"),
        P(),
        P("tile", None),
        P(),
    )
    out_specs = (P(("tile", "freq"), None), P())
    return jax.shard_map(body, mesh=mesh, in_specs=in_specs, out_specs=out_specs, check_vma=False)
```

```python
import functools
import math

import jax
import jax.numpy as jnp
import numpy as np
from jax import lax
from jax.experimental import pallas as pl
from jax.experimental.pallas import tpu as pltpu
from jax.sharding import PartitionSpec as P

HIGH = lax.Precision.HIGHEST
PHASE_RATE = 0.37
STEP_LENGTH = 0.5
EPSILON = 1e-06
MESH = pl.DeviceIdType.MESH
NX, NZ, NT = 4, 8, 8
NF = NX * NZ
ROWS = 8
F32, BF16 = jnp.float32, jnp.bfloat16
EARLY = range(NZ, 3 * NZ)
FAR_FIRST = sorted(range(1, NF), key=lambda i: (-min(i % NZ, NZ - i % NZ), -min(i // NZ, NX - i // NZ), i))
STAGES = ((0, 1, 0, 2), (1, 1, 6, 7), (2, 1, 4, 5))
NEAR_Z, FAR_Z, ALONG_X = [1, 2, NZ - 2, NZ - 1], [3, 4, 5], [NZ, 2 * NZ, 3 * NZ]


def kernel_table(freqs, samples):
    freq_col = np.arange(freqs, dtype=np.float32)[:, None] + np.float32(0.5)
    time_row = np.arange(samples, dtype=np.float32)[None, :] + np.float32(0.5)
    phases = ((np.float32(PHASE_RATE) * freq_col) * time_row).astype(np.float64)
    table = np.stack([np.cos(phases), np.sin(phases)], axis=1) / math.sqrt(freqs)
    return table.reshape(2 * freqs, samples).astype(np.float32)


def nn(a, b, precision=None):
    return lax.dot_general(a, b, (((1,), (0,)), ((), ())), precision=precision, preferred_element_type=F32)


def nt(a, b, precision=None):
    return lax.dot_general(a, b, (((1,), (1,)), ((), ())), precision=precision, preferred_element_type=F32)


def split(a):
    high = a.astype(BF16)
    return high, (a - high.astype(F32)).astype(BF16)


def three(dot, a, b):
    return dot(a[0], b[0]) + dot(a[0], b[1]) + dot(a[1], b[0])


def iota(shape, dim):
    return lax.broadcasted_iota(jnp.int32, shape, dim)


def await_bytes(ref, sem):
    pltpu.make_async_copy(ref, ref, sem).wait()


def kernel(
    wave_in, gate_in, sens_ref, models_in, obs_in, cell_in, table_in,
    gradient_ref, final_ref,
    wave_ref, gate_ref, models_ref, obs_ref, cell_ref, table_ref,
    buf, tiles, gathered, wide, expanded, onehot, model_t, rows_ref, cells_t, major, major_x, major_sum, major_z,
    minor, minor_z, minor_sum, minor_x,
    shared, partner_row, partners,
    square_row, square_rows, misfit_row, misfit_tiles, misfit_sum, misfit_rows,
    bulk_send, bulk_recv, send, recv, pair_send, pair_recv, load, known, ring_send, ring_recv,
):
    tile = lax.axis_index("tile")
    f = lax.axis_index("freq")
    x, z = f // NZ, lax.rem(f, NZ)
    chunks = buf.shape[0]
    soundings = chunks * ROWS
    gates = obs_ref.shape[1]

    def plane(i):
        return {"freq": lax.rem(x + i // NZ, NX) * NZ + lax.rem(z + i % NZ, NZ)}

    def other_tile(i):
        return {"tile": lax.rem(tile + i, NT)}

    def put(src, dst, send_sem, recv_sem, device):
        pltpu.make_async_remote_copy(
            src_ref=src, dst_ref=dst, send_sem=send_sem, recv_sem=recv_sem, device_id=device, device_id_type=MESH
        ).start()

    loads = [
        pltpu.make_async_copy(src, dst, load.at[i])
        for i, (src, dst) in enumerate((
            (models_in, models_ref), (cell_in, cell_ref), (gate_in, gate_ref),
            (wave_in, wave_ref), (table_in, table_ref), (obs_in.at[0], obs_ref),
        ))
    ]
    for copy in loads:
        copy.start()
    barrier = pltpu.get_barrier_semaphore()
    for i in NEAR_Z + ALONG_X:
        pl.semaphore_signal(barrier, inc=1, device_id=plane(i), device_id_type=MESH)
    for i in range(1, NT):
        pl.semaphore_signal(barrier, inc=1, device_id=other_tile(i), device_id_type=MESH)
    loads[0].wait()
    pl.semaphore_wait(barrier, len(NEAR_Z + ALONG_X) + NT - 1)

    for i in range(1, NT):
        put(models_ref, tiles.at[tile], send.at[0], recv.at[0], other_tile(i))

    def send_chunk(c, peers=range(1, NF)):
        for i in peers:
            p = plane(i)
            start = pl.multiple_of(p["freq"] * soundings + c * ROWS, ROWS)
            put(sens_ref.at[0, 0, :, pl.ds(start, ROWS), :], buf.at[c, f], bulk_send.at[c], bulk_recv.at[c, int(i not in EARLY)], p)

    def keep_chunk(c):
        start = pl.multiple_of(f * soundings + c * ROWS, ROWS)
        pltpu.make_async_copy(sens_ref.at[0, 0, :, pl.ds(start, ROWS), :], buf.at[c, f], bulk_recv.at[c, 1]).start()

    send_chunk(0, NEAR_Z + ALONG_X)
    for i in (2, NZ - 2):
        pl.semaphore_signal(known.at[0], inc=1, device_id=plane(i), device_id_type=MESH)
    pl.semaphore_wait(known.at[0], 2)
    for i in ALONG_X:
        pl.semaphore_signal(known.at[1], inc=1, device_id=plane(i), device_id_type=MESH)
    send_chunk(0, FAR_Z)
    pl.semaphore_wait(known.at[1], len(ALONG_X))
    send_chunk(0, [i for i in range(1, NF) if i not in NEAR_Z + ALONG_X + FAR_Z])
    for c in range(chunks):
        keep_chunk(c)

    for copy in loads[1:]:
        copy.wait()
    cells = cell_ref[...]
    block = lax.shift_right_logical(cells, 8)
    partner = jnp.max(jnp.where(block != tile, block, -1), axis=1, keepdims=True)
    local = jnp.where(block == tile, cells & 255, 256 + (cells & 255))
    ncell = cells.shape[1]
    onehot[...] = jnp.where(iota((ncell, ncell), 0) == local, 1.0, 0.0).astype(BF16)

    partner_row[...] = jnp.broadcast_to(partner.astype(F32), partner_row.shape)
    for i in range(1, NT):
        put(partner_row, partners.at[tile], send.at[6], recv.at[6], other_tile(i))
    partners[tile] = partner_row[...]
    tiles[tile] = models_ref[...]
    await_bytes(tiles.at[pl.ds(0, NT - 1)], recv.at[0])
    borrowed = jnp.zeros_like(models_ref)
    for t in range(NT):
        borrowed = jnp.where(partner == t, tiles[t], borrowed)
    gathered[x, z, 0] = models_ref[...]
    gathered[x, z, 1] = borrowed

    def pass_on(step):
        down, up = lax.rem(z - step + 1 + NZ, NZ), lax.rem(z + step - 1, NZ)
        for to, block_z, part in ((1, down, 0), (NZ - 1, up, 1)):
            block_ref = gathered.at[x, block_z] if 2 * step < NZ else gathered.at[x, block_z, part]
            put(block_ref, block_ref, ring_send.at[step - 1], ring_recv.at[step - 1], plane(to))

    def passed(step, sems):
        await_bytes(gathered.at[0, pl.ds(0, 2)] if 2 * step < NZ else gathered.at[0, 0], sems.at[step - 1])

    pass_on(1)
    first, second = EARLY, [i for i in FAR_FIRST if i not in EARLY]
    send_chunk(1, first)

    samples = table_ref.shape[1]
    rows = iota((gates, samples), 0)
    lag = lax.fori_loop(0, gates, lambda g, a: jnp.where(rows == g, gate_ref[g], a), jnp.zeros((gates, samples), jnp.int32))
    lag = lag - iota((gates, samples), 1)
    toeplitz = lax.fori_loop(
        0, samples, lambda k, a: jnp.where(lag == k, wave_ref[k], a), jnp.zeros((gates, samples), F32)
    )
    narrow = nt(toeplitz, table_ref[...], HIGH)
    spread = jnp.where(lax.shift_right_logical(iota((gates * ROWS, gates), 0), 3) == iota((gates * ROWS, gates), 1), 1.0, 0.0)
    fps = narrow.shape[1]
    pick = jnp.where(iota((fps, fps * ROWS), 0) == lax.shift_right_logical(iota((fps, fps * ROWS), 1), 3), 1.0, 0.0)
    big = nn(nn(spread, narrow, HIGH), pick, HIGH)
    same = (iota(big.shape, 0) & 7) == (iota(big.shape, 1) & 7)
    big_high, big_low = split(jnp.where(same, big, 0.0))
    wide[0] = big_high
    wide[1] = big_low
    expanded[...] = nt(spread, obs_ref[...], HIGH)

    passed(1, ring_recv)
    pass_on(2)
    send_chunk(1, second)
    passed(2, ring_recv)
    pass_on(3)
    send_chunk(2, first)
    passed(3, ring_recv)
    pass_on(4)
    send_chunk(2, second)
    passed(4, ring_recv)
    for i in range(1, NX):
        put(gathered.at[x], gathered.at[x], send.at[2], recv.at[2], plane(i * NZ))
    send_chunk(3, sorted(FAR_FIRST, key=lambda i: i not in EARLY))

    await_bytes(gathered.at[pl.ds(0, NX - 1)], recv.at[2])
    for b in range(2):
        part = gathered[:, :, b].reshape(NF * ROWS, -1)
        part_high, part_low = split(part.T)
        hot = onehot[pl.ds(b * NF * ROWS, NF * ROWS), :]
        if b == 0:
            model_high, model_low = nn(part_high, hot), nn(part_low, hot)
        else:
            model_high, model_low = model_high + nn(part_high, hot), model_low + nn(part_low, hot)
    model_t[0] = model_high.astype(BF16)
    model_t[1] = model_low.astype(BF16)

    cells_t[...] = jnp.zeros_like(cells_t)
    misfit_row[...] = jnp.zeros_like(misfit_row)

    rows_ref[...] = jnp.zeros_like(rows_ref)

    def add_squares():
        rows_t = rows_ref[...]
        misfit_row[...] += nt(jnp.ones((8, rows_t.shape[1]), F32), rows_t * rows_t, HIGH)[0:1]

    def chunk(c, carry):
        add_squares()
        seen = expanded[...]
        seen = jnp.where(iota(seen.shape, 1) == c * ROWS + (iota(seen.shape, 0) & 7), seen, 0.0)
        seen_row = nt(jnp.ones((8, seen.shape[1]), F32), seen, HIGH)[0:1]
        operator = None
        for late, offsets in enumerate(((1, 2), (3, 0))):
            await_bytes(buf.at[c, pl.ds(0, NF // 2)], bulk_recv.at[c, late])
            blocks, columns = [], [[], []]
            for offset in offsets:
                source = lax.rem(x - offset + NX, NX)
                width = NZ * 2 * ROWS
                blocks.append(buf[c, pl.ds(source * NZ, NZ)].reshape(width, ncell))
                for k in range(2):
                    columns[k].append(wide[k, :, pl.ds(pl.multiple_of(source * width, width), width)])
            block_s = split(jnp.concatenate(blocks, axis=0))
            part = three(nn, [jnp.concatenate(cols, axis=1) for cols in columns], block_s)
            operator = part if operator is None else operator + part
        operator = split(operator)
        rows_t = three(nt, (model_t[0], model_t[1]), operator) - seen_row
        rows_ref[...] = rows_t
        cells_t[...] += three(nn, split(rows_t), operator)
        return carry

    lax.fori_loop(0, chunks, chunk, 0)

    grad_high, grad_low = split(cells_t[...])
    half, lanes = NF * ROWS, cells_t.shape[0] // 2

    def global_rows(b):
        hot = onehot[pl.ds(b * half, half), :]
        return (nt(hot, grad_high) + nt(hot, grad_low)).reshape(NX, NZ, ROWS, -1)

    lent = global_rows(1)
    for q in range(2):
        major[:, q] = lent[..., q * lanes:(q + 1) * lanes]
        for i in (2, 1, 3):
            p = lax.rem(x + i, NX)
            sem = STAGES[q][2]
            put(major.at[p, q], major_x.at[x, q], pair_send.at[sem], pair_recv.at[sem], plane(i * NZ))
    own = global_rows(0)
    minor[...] = jnp.swapaxes(own[..., lanes:], 0, 1)
    for i in (4, 3, 5, 2, 6, 1, 7):
        p = lax.rem(z + i, NZ)
        put(minor.at[p], minor_z.at[z], pair_send.at[1], pair_recv.at[1], plane(i))
    major[:, 2] = own[..., :lanes]
    for i in (2, 1, 3):
        p = lax.rem(x + i, NX)
        put(major.at[p, 2], major_x.at[x, 2], pair_send.at[4], pair_recv.at[4], plane(i * NZ))
    add_squares()
    for i in range(1, NT):
        put(misfit_row, misfit_tiles.at[tile], send.at[7], recv.at[7], other_tile(i))

    major_x[x] = major[x]
    minor_z[z] = minor[z]
    for first, count, sem_x, sem_z in STAGES:
        quarters = pl.ds(first, count)
        await_bytes(major_x.at[pl.ds(0, NX - 1), quarters], pair_recv.at[sem_x])
        total_x = (major_x[0, quarters] + major_x[1, quarters]) + (major_x[2, quarters] + major_x[3, quarters])
        major_sum[:, quarters] = jnp.swapaxes(total_x, 0, 1)
        for i in (4, 3, 5, 2, 6, 1, 7):
            p = lax.rem(z + i, NZ)
            put(major_sum.at[p, quarters], major_z.at[z, quarters], pair_send.at[sem_z], pair_recv.at[sem_z], plane(i))
    await_bytes(minor_z.at[pl.ds(0, NZ - 1)], pair_recv.at[1])
    minor_sum[...] = jnp.sum(minor_z[...], axis=0)
    for i in (2, 1, 3):
        p = lax.rem(x + i, NX)
        put(minor_sum.at[p], minor_x.at[x], pair_send.at[3], pair_recv.at[3], plane(i * NZ))
    minor_x[x] = minor_sum[x]
    major_z[z] = major_sum[z]
    for q in range(2):
        await_bytes(major_z.at[pl.ds(0, NZ - 1), pl.ds(q, 1)], pair_recv.at[STAGES[q][3]])
    lent_z = jnp.sum(major_z[:, pl.ds(0, 2)], axis=0)
    shared[tile, 1, :, pl.ds(0, lanes)] = lent_z[0]
    shared[tile, 1, :, pl.ds(lanes, lanes)] = lent_z[1]
    for i in range(1, NT):
        put(shared.at[tile, 1], shared.at[tile, 1], send.at[8], recv.at[8], other_tile(i))
    await_bytes(minor_x.at[pl.ds(0, NX - 1)], pair_recv.at[3])
    shared[tile, 0, :, pl.ds(lanes, lanes)] = (minor_x[0] + minor_x[1]) + (minor_x[2] + minor_x[3])
    await_bytes(major_z.at[pl.ds(0, NZ - 1), pl.ds(2, 1)], pair_recv.at[STAGES[2][3]])
    shared[tile, 0, :, pl.ds(0, lanes)] = jnp.sum(major_z[:, 2], axis=0)
    for i in range(1, NT):
        put(shared.at[tile, 0], shared.at[tile, 0], send.at[4], recv.at[4], other_tile(i))
    misfit_tiles[tile] = misfit_row[...]
    await_bytes(misfit_tiles.at[pl.ds(0, NT - 1)], recv.at[7])
    misfit_sum[...] = jnp.sum(misfit_tiles[...], axis=0)
    for i in range(1, NF):
        put(misfit_sum, misfit_rows.at[f], send.at[3], recv.at[3], plane(i))
    await_bytes(partners.at[pl.ds(0, NT - 1)], recv.at[6])
    await_bytes(shared.at[pl.ds(0, NT - 1), 1], recv.at[8])
    await_bytes(shared.at[pl.ds(0, NT - 1), 0], recv.at[4])

    def gradient_of(t, own_rows):
        for lender in range(NT):
            own_rows = own_rows + jnp.where(partners[lender][:, 0:1] == t, shared[lender, 1], 0.0)
        return own_rows

    squares = jnp.zeros_like(models_ref)
    for t in range(NT):
        rows_of = gradient_of(float(t), shared[t, 0])
        squares = squares + rows_of * rows_of
    square_row[...] = jnp.sum(squares, axis=0, keepdims=True)
    for i in FAR_FIRST:
        put(square_row, square_rows.at[f], send.at[5], recv.at[5], plane(i))
    gradient_ref[...] = gradient_of(tile.astype(F32), shared[tile, 0])
    square_rows[f] = square_row[...]
    misfit_rows[f] = misfit_sum[...]
    await_bytes(misfit_rows.at[pl.ds(0, NF - 1)], recv.at[3])
    members = misfit_row.shape[1]
    final_ref[:, pl.ds(members, members)] = jnp.sum(misfit_rows[...], axis=0)
    await_bytes(square_rows.at[pl.ds(0, NF - 1)], recv.at[5])
    final_ref[:, pl.ds(0, members)] = jnp.sum(square_rows[...], axis=0)

    for c in range(chunks):
        await_bytes(buf.at[c, pl.ds(0, NF - 1)], bulk_send.at[c])
    await_bytes(tiles.at[pl.ds(0, NT - 1)], send.at[0])
    for step in range(1, NZ // 2 + 1):
        passed(step, ring_send)
    await_bytes(gathered.at[pl.ds(0, NX - 1)], send.at[2])
    await_bytes(misfit_rows.at[pl.ds(0, NF - 1)], send.at[3])
    await_bytes(shared.at[pl.ds(0, NT - 1), 1], send.at[8])
    await_bytes(shared.at[pl.ds(0, NT - 1), 0], send.at[4])
    await_bytes(misfit_tiles.at[pl.ds(0, NT - 1)], send.at[7])
    await_bytes(square_rows.at[pl.ds(0, NF - 1)], send.at[5])
    await_bytes(partners.at[pl.ds(0, NT - 1)], send.at[6])
    for first, count, sem_x, sem_z in STAGES:
        await_bytes(major_x.at[pl.ds(0, NX - 1), pl.ds(first, count)], pair_send.at[sem_x])
        await_bytes(major_z.at[pl.ds(0, NZ - 1), pl.ds(first, count)], pair_send.at[sem_z])
    await_bytes(minor_z.at[pl.ds(0, NZ - 1)], pair_send.at[1])
    await_bytes(minor_x.at[pl.ds(0, NX - 1)], pair_send.at[3])


def finish(total, ncells, models_ref, gradient_ref, final_ref, out_ref, misfit_ref):
    members = models_ref.shape[1]
    misfit = final_ref[:, pl.ds(members, members)] / (2.0 * total)
    scale = jnp.sqrt(final_ref[:, pl.ds(0, members)] / ncells + EPSILON)
    out_ref[...] = models_ref[...] - STEP_LENGTH * (misfit / scale) * gradient_ref[...]
    misfit_ref[...] = misfit


def body(sensitivity, models, observed, waveform, cell_index, gate_index):
    owned, members = models.shape
    gates = gate_index.shape[0]
    ncell = cell_index.shape[1]
    chunks = sensitivity.shape[3] // NF // ROWS
    table = jnp.asarray(kernel_table(NF, waveform.shape[0]))
    hbm, vmem = pl.BlockSpec(memory_space=pl.ANY), pl.BlockSpec(memory_space=pltpu.VMEM)
    dma = pltpu.SemaphoreType.DMA
    gradient, final = pl.pallas_call(
        kernel,
        out_shape=(jax.ShapeDtypeStruct((owned, members), F32), jax.ShapeDtypeStruct((1, 2 * members), F32)),
        in_specs=[hbm] * 7,
        out_specs=(vmem, vmem),
        scratch_shapes=[
            pltpu.SMEM(waveform.shape, F32),
            pltpu.SMEM(gate_index.shape, jnp.int32),
            pltpu.VMEM(models.shape, F32),
            pltpu.VMEM((observed.shape[2], gates), F32),
            pltpu.VMEM(cell_index.shape, jnp.int32),
            pltpu.VMEM(table.shape, F32),
            pltpu.VMEM((chunks, NF, 2, ROWS, ncell), F32),
            pltpu.VMEM((NT, ROWS, members), F32),
            pltpu.VMEM((NX, NZ, 2, ROWS, members), F32),
            pltpu.VMEM((2, gates * ROWS, 2 * NF * ROWS), BF16),
            pltpu.VMEM((gates * ROWS, chunks * ROWS), F32),
            pltpu.VMEM((ncell, ncell), BF16),
            pltpu.VMEM((2, members, ncell), BF16),
            pltpu.VMEM((members, gates * ROWS), F32),
            pltpu.VMEM((members, ncell), F32),
            pltpu.VMEM((NX, 3, NZ, ROWS, members // 2), F32),
            pltpu.VMEM((NX, 3, NZ, ROWS, members // 2), F32),
            pltpu.VMEM((NZ, 3, ROWS, members // 2), F32),
            pltpu.VMEM((NZ, 3, ROWS, members // 2), F32),
            pltpu.VMEM((NZ, NX, ROWS, members // 2), F32),
            pltpu.VMEM((NZ, NX, ROWS, members // 2), F32),
            pltpu.VMEM((NX, ROWS, members // 2), F32),
            pltpu.VMEM((NX, ROWS, members // 2), F32),
            pltpu.VMEM((NT, 2, ROWS, members), F32),
            pltpu.VMEM((1, 128), F32),
            pltpu.VMEM((NT, 1, 128), F32),
            pltpu.VMEM((1, members), F32),
            pltpu.VMEM((NF, 1, members), F32),
            pltpu.VMEM((1, members), F32),
            pltpu.VMEM((NT, 1, members), F32),
            pltpu.VMEM((1, members), F32),
            pltpu.VMEM((NF, 1, members), F32),
            dma((chunks,)), dma((chunks, 2)), dma((9,)), dma((9,)), dma((8,)), dma((8,)), dma((6,)), pltpu.SemaphoreType.REGULAR((2,)), dma((NZ // 2,)), dma((NZ // 2,)),
        ],
        compiler_params=pltpu.CompilerParams(collective_id=0, has_side_effects=True, vmem_limit_bytes=60 << 20),
    )(waveform, gate_index, sensitivity, models, jnp.swapaxes(observed, 1, 2), cell_index, table)
    devices = NT * NF
    updated, misfit = pl.pallas_call(
        functools.partial(finish, NT * sensitivity.shape[3] * gates, owned * devices),
        out_shape=(jax.ShapeDtypeStruct((owned, members), F32), jax.ShapeDtypeStruct((1, members), F32)),
        in_specs=[vmem] * 3,
        out_specs=(vmem, vmem),
    )(models, gradient, final)
    return updated, misfit[0]


def solution(mesh):
    in_specs = (
        P("tile", "freq", None, None, None),
        P(("tile", "freq"), None),
        P("tile", None, "freq"),
        P(),
        P("tile", None),
        P(),
    )
    out_specs = (P(("tile", "freq"), None), P())
    return jax.shard_map(body, mesh=mesh, in_specs=in_specs, out_specs=out_specs, check_vma=False)
```
